32 devices in a mesh: dp: 8 (over z, y), tensor: 4 (over x, core).
Axes of the slice: x: 2, y: 2, z: 4, core: 2. Of those that a mesh axis runs over, the one named last changes fastest.
Arguments:
- tokens: bfloat16 [8192, 2048], P('dp'), may hold values from -6 to 6
- segment_ids: int32 [8, 1024], P('dp'), may hold values from 0 to 7, never falling along the last dimension, each value on 1 to 512 neighbouring positions
- attn_gain: bfloat16 [2048], P('dp'), may hold values from 0.25 to 1.75
- query_weight: bfloat16 [2048, 2048], P('dp', 'tensor'), may hold values from -0.125 to 0.125
- key_weight: bfloat16 [2048, 512], P('dp', 'tensor'), may hold values from -0.125 to 0.125
- value_weight: bfloat16 [2048, 512], P('dp', 'tensor'), may hold values from -0.125 to 0.125
- output_weight: bfloat16 [2048, 2048], P('tensor', 'dp'), may hold values from -0.5 to 0.5
- ffn_gain: bfloat16 [2048], P('dp'), may hold values from 0.25 to 1.75
- gate_weight: bfloat16 [2048, 8192], P('dp', 'tensor'), may hold values from -0.125 to 0.125
- up_weight: bfloat16 [2048, 8192], P('dp', 'tensor'), may hold values from -0.125 to 0.125
- down_weight: bfloat16 [8192, 2048], P('tensor', 'dp'), may hold values from -0.0625 to 0.0625
- cotangent: bfloat16 [8192, 2048], P('dp'), may hold values from -6 to 6
Outputs:
- layer_output: bfloat16 [8192, 2048], P('dp')
- tokens_grad: float32 [8192, 2048], P('dp')
- attn_gain_grad: float32 [2048], P('dp')
- query_weight_grad: float32 [2048, 2048], P('dp', 'tensor')
- key_weight_grad: float32 [2048, 512], P('dp', 'tensor')
- value_weight_grad: float32 [2048, 512], P('dp', 'tensor')
- output_weight_grad: float32 [2048, 2048], P('tensor', 'dp')
- ffn_gain_grad: float32 [2048], P('dp')
- gate_weight_grad: float32 [2048, 8192], P('dp', 'tensor')
- up_weight_grad: float32 [2048, 8192], P('dp', 'tensor')
- down_weight_grad: float32 [8192, 2048], P('tensor', 'dp')
The draws below stay inside these ranges and needn't reach their ends.
Inputs may be any that keep to these rules, and one draw needn't show every extreme that they name: In each row of segment_ids the numbers never fall; each document spans 1 to 512 positions, and one spans exactly 512.
All inputs are finite; a program needn't handle non-finite values.
Results may differ from the reference program's by a relative error of at most 0.02.
Values may be sent and summed in bfloat16 or wider, within the bound.
A program may use at most 256 MiB of HBM per device.

```python
import math
from functools import partial
import jax
import jax.numpy as jnp
import numpy as np
from jax import lax

D = 2048
HEADS = 32
KV = 8
HD = 64
FF = 8192
GROUP = 4
LENGTH = 1024
DOCS = 8
MOST = 512
SEQS = 8
TOKENS = 8192


def shard_levels(key, shape, split, least, top_value):
    def one(dim, blocks):
        draws = jax.random.uniform(jax.random.fold_in(jax.random.fold_in(key, 6), dim), (blocks,), jnp.float32, least / len(split), top_value / len(split))
        return jnp.repeat(jnp.exp(draws), shape[dim] // blocks).reshape((-1,) + (1,) * (len(shape) - dim - 1))

    factor_of = one(*split[0])
    for cut in split[1:]:
        factor_of = factor_of * one(*cut)
    return factor_of


def profile(amount, total, limit, lean):
    loads = [(1 << 20) // math.isqrt(rank ** lean) + 1 for rank in range(2, amount + 1)]
    rest, holding = total - limit - (amount - 1), [1] * (amount - 1)
    while rest > 0:
        candidates = [i for i in range(amount - 1) if holding[i] < limit]
        mass, remaining = sum([loads[i] for i in candidates]), rest
        for i in candidates:
            addition = min(limit - holding[i], max(1, remaining * loads[i] // mass), rest)
            holding[i] = holding[i] + addition
            rest = rest - addition
    return np.array([limit] + holding)


def uneven_parts(key, count, total, most, skew):
    if count == 2:
        one = jax.random.randint(key, (), max(1, total - most), min(most, total - 1) + 1)
        return jnp.stack([one, total - one])
    sizes = jnp.asarray(profile(count, total, most, skew), jnp.int32)
    twos = (count - 1) // 2
    donor, sink = sizes[1:1 + 2 * twos:2], sizes[2:2 + 2 * twos:2]
    slack = jnp.minimum(donor - 1, most - sink)
    passed = jax.random.randint(jax.random.fold_in(key, 1), (twos,), 0, 1 << 20) % (slack + 1)
    sizes = sizes.at[1:1 + 2 * twos:2].set(donor - passed).at[2:2 + 2 * twos:2].set(sink + passed)
    return sizes[jax.random.permutation(jax.random.fold_in(key, 2), count)]


def bell_draw(rng, shape, scale, limit, shards=(), kind=jnp.bfloat16):
    values = scale * jax.random.normal(rng, shape, jnp.float32)
    if shards:
        values = values * shard_levels(rng, shape, shards, -0.22, 0.18)
    return jnp.clip(values, -limit, limit).astype(kind)


def setup_inputs(seed: int = 0) -> dict:
    streams_of = jax.random.split(jax.random.key(seed), 13)
    tokens = bell_draw(streams_of[0], (TOKENS, D), 1.0, 6.0, ((0, 8),))
    segment_ids = jax.vmap(lambda own: jnp.searchsorted(jnp.cumsum(uneven_parts(own, DOCS, LENGTH, MOST, 2)), jnp.arange(LENGTH), side="right"))(jax.random.split(streams_of[1], SEQS)).reshape((SEQS, LENGTH)).astype(jnp.int32)
    attn_gain = jnp.clip(1.0 + 0.15 * jax.random.normal(streams_of[2], (D,), jnp.float32), 0.25, 1.75).astype(jnp.bfloat16)
    query_weight = bell_draw(streams_of[3], (D, HEADS * HD), D ** -0.5, 0.125, ((0, 8), (1, 4)))
    key_weight = bell_draw(streams_of[4], (D, KV * HD), D ** -0.5, 0.125, ((0, 8), (1, 4)))
    value_weight = bell_draw(streams_of[5], (D, KV * HD), D ** -0.5, 0.125, ((0, 8), (1, 4)))
    output_weight = bell_draw(streams_of[6], (HEADS * HD, D), (HEADS * HD // 16) ** -0.5, 0.5, ((0, 4), (1, 8)))
    ffn_gain = jnp.clip(1.0 + 0.15 * jax.random.normal(streams_of[7], (D,), jnp.float32), 0.25, 1.75).astype(jnp.bfloat16)
    gate_weight = bell_draw(streams_of[8], (D, FF), D ** -0.5, 0.125, ((0, 8), (1, 4)))
    up_weight = bell_draw(streams_of[9], (D, FF), D ** -0.5, 0.125, ((0, 8), (1, 4)))
    down_weight = bell_draw(streams_of[10], (FF, D), FF ** -0.5, 0.0625, ((0, 4), (1, 8)))
    cotangent = bell_draw(streams_of[11], (TOKENS, D), 1.0, 6.0, ((0, 8),))
    return {"tokens": tokens, "segment_ids": segment_ids, "attn_gain": attn_gain, "query_weight": query_weight, "key_weight": key_weight, "value_weight": value_weight, "output_weight": output_weight, "ffn_gain": ffn_gain, "gate_weight": gate_weight, "up_weight": up_weight, "down_weight": down_weight, "cotangent": cotangent}


@jax.custom_vjp
def low(v):
    return lax.optimization_barrier(v.astype(jnp.bfloat16)).astype(jnp.float32)

@jax.custom_vjp
def low_back(v):
    return v

def low_keep(v):
    return (low(v), None)

def low_pass(kept, grad):
    return (grad,)

def back_keep(v):
    return (v, None)

def back_low(kept, grad):
    return (low(grad),)
low.defvjp(low_keep, low_pass)
low_back.defvjp(back_keep, back_low)
epsilon = 1e-05
highest = lax.Precision.HIGHEST

def rope_tables(segment_row, head_size):
    length = segment_row.shape[0]
    places = jnp.arange(length, dtype=jnp.int32)
    boundary = jnp.concatenate([jnp.ones((1,), dtype=bool), segment_row[1:] != segment_row[:-1]])
    starts = lax.cummax(jnp.where(boundary, places, 0), axis=0)
    position = (places - starts).astype(jnp.float32)
    half_size = head_size // 2
    exponent = jnp.arange(half_size, dtype=jnp.float32) * 2.0 / head_size
    inverse = 1.0 / 500000.0 ** exponent
    wavelen = 2.0 * math.pi / inverse
    smooth = (8192.0 / wavelen - 1.0) / 3.0
    scaled = jnp.where(wavelen < 2048.0, inverse, jnp.where(wavelen > 8192.0, inverse / 32.0, (1.0 - smooth) * inverse / 32.0 + smooth * inverse))
    angles = position[:, None] * scaled[None, :]
    cosine_table = jnp.cos(angles)
    sine_table = jnp.sin(angles)
    return (jnp.concatenate([cosine_table, cosine_table], axis=-1), jnp.concatenate([sine_table, sine_table], axis=-1))

def rotate(values, cosine_table, sine_table):
    half_size = values.shape[-1] // 2
    turned = jnp.concatenate([-values[..., half_size:], values[..., :half_size]], axis=-1)
    return values * cosine_table + turned * sine_table

def rms_norm(values, gain_vector):
    factor = lax.rsqrt(lax.optimization_barrier(jnp.mean(values * values, axis=-1, keepdims=True)) + epsilon)
    return values * factor * gain_vector

def matmul(left_side, right_side):
    return jnp.dot(left_side, right_side, precision=highest)

def attend_one(operands):
    query_seq, key_seq, value_seq, segment_row = operands
    length = key_seq.shape[0]
    grouped = query_seq.reshape(length, KV, GROUP, HD)
    scores = jnp.einsum('qkgd,skd->kgqs', grouped, key_seq, precision=highest) * HD ** (-0.5)
    scores = low_back(scores)
    places = jnp.arange(length, dtype=jnp.int32)
    same_doc = segment_row[:, None] == segment_row[None, :]
    allowed = same_doc & (places[None, :] <= places[:, None])
    scores = jnp.where(allowed, scores, -1000000000.0)
    row_max = lax.optimization_barrier(jnp.max(scores, axis=-1, keepdims=True))
    log_total = jnp.log(lax.optimization_barrier(jnp.sum(jnp.exp(scores - row_max), axis=-1, keepdims=True))) + row_max
    soft_low = low(jnp.exp(scores - log_total))
    mixed_seq = jnp.einsum('kgqs,skd->qkgd', soft_low, value_seq, precision=highest)
    return mixed_seq.reshape(length, HEADS * HD)

def reference(tokens, segment_ids, attn_gain, query_weight, key_weight, value_weight, output_weight, ffn_gain, gate_weight, up_weight, down_weight, cotangent):
    cosine_table, sine_table = jax.vmap(partial(rope_tables, head_size=HD))(segment_ids)
    cosine_wide = cosine_table[:, :, None, :]
    sine_wide = sine_table[:, :, None, :]

    def forward(tokens_float, attn_scale, query_matrix, key_matrix, value_matrix, output_matrix, ffn_scale, gate_matrix, up_matrix, down_matrix):
        normed = low(rms_norm(tokens_float, attn_scale))
        query_raw = low_back(matmul(normed, query_matrix)).reshape(SEQS, LENGTH, HEADS, HD)
        key_raw = low_back(matmul(normed, key_matrix)).reshape(SEQS, LENGTH, KV, HD)
        value_seqs = low(low_back(matmul(normed, value_matrix))).reshape(SEQS, LENGTH, KV, HD)
        query_seqs = low(rotate(query_raw, cosine_wide, sine_wide))
        key_seqs = low(rotate(key_raw, cosine_wide, sine_wide))
        mixed = lax.map(jax.checkpoint(attend_one), (query_seqs, key_seqs, value_seqs, segment_ids))
        mixed = low(low_back(mixed.reshape(TOKENS, HEADS * HD)))
        hidden_state = tokens_float + low_back(matmul(mixed, output_matrix))
        normed_two = low(rms_norm(hidden_state, ffn_scale))
        gate_values = low_back(matmul(normed_two, gate_matrix))
        up_values = low_back(matmul(normed_two, up_matrix))
        active = low(jax.nn.silu(gate_values) * up_values)
        return hidden_state + low_back(matmul(active, down_matrix))
    result, pullback = jax.vjp(forward, tokens.astype(jnp.float32), attn_gain.astype(jnp.float32), query_weight.astype(jnp.float32), key_weight.astype(jnp.float32), value_weight.astype(jnp.float32), output_weight.astype(jnp.float32), ffn_gain.astype(jnp.float32), gate_weight.astype(jnp.float32), up_weight.astype(jnp.float32), down_weight.astype(jnp.float32))
    grads = pullback(cotangent.astype(jnp.float32))
    return (result.astype(jnp.bfloat16), grads[0], grads[1], grads[2], grads[3], grads[4], grads[5], grads[6], grads[7], grads[8], grads[9])
```

```python
from functools import partial
import math

import jax
import jax.numpy as jnp
from jax import lax
from jax.sharding import PartitionSpec as P

HD = 64
GROUP = 4
epsilon = 1e-05
BF = jnp.bfloat16
F32 = jnp.float32


def rope_tables(segment_row, head_size):
    length = segment_row.shape[0]
    places = jnp.arange(length, dtype=jnp.int32)
    boundary = jnp.concatenate([jnp.ones((1,), dtype=bool), segment_row[1:] != segment_row[:-1]])
    starts = lax.cummax(jnp.where(boundary, places, 0), axis=0)
    position = (places - starts).astype(jnp.float32)
    half_size = head_size // 2
    exponent = jnp.arange(half_size, dtype=jnp.float32) * 2.0 / head_size
    inverse = 1.0 / 500000.0**exponent
    wavelen = 2.0 * math.pi / inverse
    smooth = (8192.0 / wavelen - 1.0) / 3.0
    scaled = jnp.where(
        wavelen < 2048.0,
        inverse,
        jnp.where(
            wavelen > 8192.0, inverse / 32.0, (1.0 - smooth) * inverse / 32.0 + smooth * inverse
        ),
    )
    angles = position[:, None] * scaled[None, :]
    cosine_table = jnp.cos(angles)
    sine_table = jnp.sin(angles)
    return (
        jnp.concatenate([cosine_table, cosine_table], axis=-1),
        jnp.concatenate([sine_table, sine_table], axis=-1),
    )


def rotate(values, cosine_table, sine_table):
    half_size = values.shape[-1] // 2
    turned = jnp.concatenate([-values[..., half_size:], values[..., :half_size]], axis=-1)
    return values * cosine_table + turned * sine_table


def dot_rows(left, right, out=F32):
    return lax.dot_general(
        left, right, (((0,), (0,)), ((), ())), preferred_element_type=F32
    ).astype(out)


def dot_cols(left, right, out=F32):
    return lax.dot_general(
        left, right, (((1,), (1,)), ((), ())), preferred_element_type=F32
    ).astype(out)


def dot(left, right, out=F32):
    return jnp.dot(left, right, preferred_element_type=F32).astype(out)


def tie(value, *others):
    return lax.optimization_barrier((value, *others))[0]


def inverse_root(values):
    return lax.rsqrt(jnp.mean(values * values, axis=-1, keepdims=True) + epsilon)


def block_scores(query_block, key_seq, segment_row, start_row):
    row_count = query_block.shape[0]
    length = key_seq.shape[0]
    scores = jnp.einsum("qkgd,skd->kgqs", query_block, key_seq, preferred_element_type=F32)
    row_ids = start_row + jnp.arange(row_count, dtype=jnp.int32)
    col_ids = jnp.arange(length, dtype=jnp.int32)
    same_doc = segment_row[start_row : start_row + row_count][:, None] == segment_row[None, :]
    allowed = same_doc & (col_ids[None, :] <= row_ids[:, None])
    return jnp.where(allowed, scores, -1000000000.0)


def attend_forward(query_seq, key_seq, value_seq, segment_row):
    length, kv_local, head_size = key_seq.shape
    grouped = query_seq.reshape(length, kv_local, -1, head_size)
    block_rows = min(512, length)
    mixed_parts = []
    total_parts = []
    for start_row in range(0, length, block_rows):
        scores = block_scores(
            grouped[start_row : start_row + block_rows], key_seq, segment_row, start_row
        )
        row_max = jnp.max(scores, axis=-1, keepdims=True)
        log_total = jnp.log(jnp.sum(jnp.exp(scores - row_max), axis=-1, keepdims=True)) + row_max
        soft_low = jnp.exp(scores - log_total).astype(BF)
        mixed_block = jnp.einsum("kgqs,skd->qkgd", soft_low, value_seq, preferred_element_type=F32)
        mixed_parts.append(mixed_block.reshape(block_rows, -1).astype(BF))
        total_parts.append(log_total)
    return (jnp.concatenate(mixed_parts, axis=0), jnp.concatenate(total_parts, axis=2))


def attend_backward(query_seq, key_seq, value_seq, log_total, grad_seq, segment_row):
    length, kv_local, head_size = key_seq.shape
    grouped = query_seq.reshape(length, kv_local, -1, head_size)
    grad_grouped = grad_seq.reshape(length, kv_local, -1, head_size)
    block_rows = min(512, length)
    score_scale = head_size ** (-0.5)
    query_parts = []
    key_grad = jnp.zeros(key_seq.shape, F32)
    value_grad = jnp.zeros(value_seq.shape, F32)
    for start_row in range(0, length, block_rows):
        query_block = grouped[start_row : start_row + block_rows]
        grad_block = grad_grouped[start_row : start_row + block_rows]
        scores = block_scores(query_block, key_seq, segment_row, start_row)
        soft_weights = jnp.exp(scores - log_total[:, :, start_row : start_row + block_rows])
        soft_grad = jnp.einsum("qkgd,skd->kgqs", grad_block, value_seq, preferred_element_type=F32)
        score_grad = (
            soft_weights * (soft_grad - jnp.sum(soft_weights * soft_grad, axis=-1, keepdims=True))
        ).astype(BF)
        query_parts.append(
            jnp.einsum("kgqs,skd->qkgd", score_grad, key_seq, preferred_element_type=F32)
            * score_scale
        )
        key_grad = key_grad + jnp.einsum(
            "kgqs,qkgd->skd", score_grad, query_block, preferred_element_type=F32
        )
        value_grad = value_grad + jnp.einsum(
            "kgqs,qkgd->skd", soft_weights.astype(BF), grad_block, preferred_element_type=F32
        )
    query_grad = jnp.concatenate(query_parts, axis=0).reshape(length, -1, head_size)
    return (query_grad, key_grad, value_grad)


def shards(
    dp_size,
    tensor_size,
    tokens,
    segment_ids,
    attn_gain,
    query_weight,
    key_weight,
    value_weight,
    output_weight,
    ffn_gain,
    gate_weight,
    up_weight,
    down_weight,
    cotangent,
):
    groups = dp_size // 2
    dp_index = lax.axis_index("dp")
    z_index, y_index = dp_index // 2, dp_index % 2
    t_index = lax.axis_index("tensor")
    token_count, width = tokens.shape
    rows = query_weight.shape[0]
    quarter = token_count // tensor_size
    half_quarter = quarter // 2

    def swap_y(value):
        return lax.ppermute(value, "dp", [(i, i ^ 1) for i in range(dp_size)])

    def swap_x(value):
        return lax.ppermute(value, "tensor", [(i, i ^ 2) for i in range(tensor_size)])

    def swap_core(value):
        return lax.ppermute(value, "tensor", [(i, i ^ 1) for i in range(tensor_size)])

    def hop(value):
        return lax.ppermute(value, "dp", [(i, (i + 2) % dp_size) for i in range(dp_size)])

    def ring_gather(value):
        pieces = [value]
        for _ in range(groups - 1):
            pieces.append(hop(pieces[-1]))
        return pieces

    def place(pieces, side, axis):
        size = pieces[0][0].shape[axis]
        shape = list(pieces[0][0].shape)
        shape[axis] = size * dp_size
        whole = jnp.zeros(shape, BF)
        for value, step, y_of in pieces:
            block = ((z_index - step) % groups) * 2 + y_of
            start = [0, 0]
            start[axis] = block * size
            whole = lax.dynamic_update_slice(whole, value, tuple(start))
        return whole

    def my_half(value, axis, mine):
        size = value.shape[axis] // 2
        which = y_index if mine else 1 - y_index
        return lax.dynamic_slice_in_dim(value, which * size, size, axis)

    def relative(value):
        return jnp.concatenate(
            [
                lax.dynamic_slice_in_dim(value, (t_index ^ j) * quarter, quarter, 0)
                for j in range(tensor_size)
            ],
            axis=0,
        )

    def absolute(pieces, dtype):
        whole = jnp.zeros((quarter * tensor_size, pieces[0].shape[1]), dtype)
        for j, piece in enumerate(pieces):
            whole = lax.dynamic_update_slice(
                whole, piece.astype(dtype), ((t_index ^ j) * quarter, 0)
            )
        return whole

    attn_scale = attn_gain.astype(F32)[:, None]
    ffn_scale = ffn_gain.astype(F32)[:, None]

    def scaled(weight, scale):
        return (weight.astype(F32) * scale).astype(BF)

    qkv_local = scaled(jnp.concatenate([query_weight, key_weight, value_weight], axis=1), attn_scale)
    qkv_ring = ring_gather(qkv_local)
    qkv_other = [swap_y(v) for v in qkv_ring]
    qkv_full = place(
        [(v, s, y_index) for s, v in enumerate(qkv_ring)]
        + [(v, s, 1 - y_index) for s, v in enumerate(qkv_other)],
        None,
        0,
    )
    out_ring = ring_gather(tie(output_weight, qkv_ring[-2]))
    out_other = [swap_y(v) for v in out_ring]
    out_full = place(
        [(v, s, y_index) for s, v in enumerate(out_ring)]
        + [(v, s, 1 - y_index) for s, v in enumerate(out_other)],
        None,
        1,
    )

    gate_scaled, up_scaled = scaled(gate_weight, ffn_scale), scaled(up_weight, ffn_scale)
    gu_mine = jnp.concatenate([my_half(gate_scaled, 1, True), my_half(up_scaled, 1, True)], axis=1)
    gu_send = jnp.concatenate([my_half(gate_scaled, 1, False), my_half(up_scaled, 1, False)], axis=1)
    gu_got = swap_y(tie(gu_send, qkv_ring[1]))
    gu_ring_a = ring_gather(tie(gu_mine, out_ring[-2]))
    gu_ring_b = ring_gather(tie(gu_got, gu_ring_a[-2]))
    gu_full = place(
        [(v, s, y_index) for s, v in enumerate(gu_ring_a)]
        + [(v, s, 1 - y_index) for s, v in enumerate(gu_ring_b)],
        None,
        0,
    )
    down_got = swap_y(tie(my_half(down_weight, 0, False), gu_got))
    down_ring_a = ring_gather(tie(my_half(down_weight, 0, True), gu_ring_b[-2]))
    down_ring_b = ring_gather(tie(down_got, down_ring_a[-2]))
    down_full = place(
        [(v, s, y_index) for s, v in enumerate(down_ring_a)]
        + [(v, s, 1 - y_index) for s, v in enumerate(down_ring_b)],
        None,
        1,
    )
    cot_rel = relative(cotangent)
    cot_y = swap_y(tie(cot_rel[:quarter], down_got))
    cot_yx = swap_x(cot_y)
    cot_yc = swap_core(jnp.concatenate([cot_y, cot_yx], axis=0))
    cot_all = jnp.concatenate(
        [cot_rel, cot_y, cot_yc[:quarter], cot_yx, cot_yc[quarter:]], axis=0
    )

    tokens_float = tokens.astype(F32)
    token_root = inverse_root(tokens_float)
    normed = (tokens_float * token_root).astype(BF)
    qkv_raw = dot(normed, qkv_full)
    q_cols, kv_cols = query_weight.shape[1], key_weight.shape[1]
    segment_row = segment_ids[0]
    cosine_table, sine_table = rope_tables(segment_row, HD)
    cosine_wide, sine_wide = cosine_table[:, None, :], sine_table[:, None, :]
    query_raw = qkv_raw[:, :q_cols].reshape(token_count, -1, HD)
    key_raw = qkv_raw[:, q_cols : q_cols + kv_cols].reshape(token_count, -1, HD)
    value_seq = qkv_raw[:, q_cols + kv_cols :].astype(BF).reshape(token_count, -1, HD)
    query_low = (rotate(query_raw, cosine_wide, sine_wide) * HD ** (-0.5)).astype(BF)
    key_low = rotate(key_raw, cosine_wide, sine_wide).astype(BF)
    mixed, log_total = attend_forward(query_low, key_low, value_seq, segment_row)
    mixed_rel = relative(mixed)
    attn_part = dot(mixed_rel, out_full, BF)

    def two_way(first, second):
        return first.astype(F32) + second.astype(F32)

    def scatter_tensor(part):
        send = jnp.concatenate([part[quarter : 2 * quarter], part[3 * quarter :]], axis=0)
        got = swap_core(send)
        keep = two_way(part[:quarter], got[:quarter])
        pass_on = two_way(part[2 * quarter : 3 * quarter], got[quarter:]).astype(BF)
        return keep + swap_x(pass_on).astype(F32)

    def gather_tensor(piece):
        from_core = swap_core(piece)
        from_x = swap_x(piece)
        from_both = swap_core(from_x)
        return [piece, from_core, from_x, from_both]

    def my_quarter(value):
        return lax.dynamic_slice_in_dim(value, t_index * quarter, quarter, 0)

    tokens_quarter = my_quarter(tokens).astype(F32)
    hidden = tokens_quarter + scatter_tensor(attn_part)
    hidden_root = inverse_root(hidden)
    n_two = (hidden * hidden_root).astype(BF)

    first, second = n_two[:half_quarter], n_two[half_quarter:]
    first_x, second_y = swap_x(first), swap_y(second)
    first_y = swap_y(jnp.concatenate([first, first_x], axis=0))
    second_x = swap_x(jnp.concatenate([second, second_y], axis=0))
    held = jnp.concatenate(
        [
            first,
            second,
            first_x,
            second_x[:half_quarter],
            first_y[:half_quarter],
            second_y,
            first_y[half_quarter:],
            second_x[half_quarter:],
        ],
        axis=0,
    )
    crossed = swap_core(held)
    n_all = jnp.concatenate(
        [
            piece
            for y_side in range(2)
            for x_side in range(2)
            for piece in (
                held[(2 * y_side + x_side) * quarter : (2 * y_side + x_side + 1) * quarter],
                crossed[(2 * y_side + x_side) * quarter : (2 * y_side + x_side + 1) * quarter],
            )
        ],
        axis=0,
    )
    hidden_units = gate_weight.shape[1] // 2
    gu_values = dot(n_all, gu_full, BF)
    gate_values = gu_values[:, :hidden_units].astype(F32)
    up_values = gu_values[:, hidden_units:].astype(F32)
    sig = jax.nn.sigmoid(gate_values)
    silu = gate_values * sig
    active = (silu * up_values).astype(BF)

    def scatter_pair(part):
        blocks = [part[j * quarter : (j + 1) * quarter] for j in range(8)]
        got = swap_core(jnp.concatenate([blocks[1], blocks[3], blocks[5], blocks[7]], axis=0))
        kept = [
            two_way(blocks[2 * j], got[j * quarter : (j + 1) * quarter]) for j in range(4)
        ]
        top = [v[:half_quarter] for v in kept]
        low = [v[half_quarter:] for v in kept]
        top_got = swap_x(jnp.concatenate([top[1], top[3]], axis=0).astype(BF)).astype(F32)
        low_got = swap_y(jnp.concatenate([low[2], low[3]], axis=0).astype(BF)).astype(F32)
        top_keep = top[0] + top_got[:half_quarter]
        top_pass = (top[2] + top_got[half_quarter:]).astype(BF)
        low_keep = low[0] + low_got[:half_quarter]
        low_pass = (low[1] + low_got[half_quarter:]).astype(BF)
        return jnp.concatenate(
            [
                top_keep + swap_y(top_pass).astype(F32),
                low_keep + swap_x(low_pass).astype(F32),
            ],
            axis=0,
        )

    def ring_scatter(grad, axis):
        size = grad.shape[axis] // groups

        def block(index):
            return lax.dynamic_slice_in_dim(grad, (index % groups) * size, size, axis)

        running = block(z_index - 1)
        for step in range(groups - 1):
            received = hop(running)
            running = (received.astype(F32) + block(z_index - 2 - step).astype(F32)).astype(BF)
        return running

    down_grad = dot_rows(active, cot_all, BF)
    down_block = ring_scatter(down_grad, 1)

    active_grad = dot_cols(cot_all, down_full)
    gate_grad = (active_grad * up_values * (sig * (1.0 + gate_values * (1.0 - sig)))).astype(BF)
    up_grad = (active_grad * silu).astype(BF)
    gu_grad = jnp.concatenate([gate_grad, up_grad], axis=1)
    e_part = dot_cols(gu_grad, gu_full, BF)
    e_two = scatter_pair(e_part)
    n_hidden = hidden * hidden_root
    cot_quarter = my_quarter(cotangent).astype(F32)
    hidden_grad = cot_quarter + hidden_root * (
        e_two - n_hidden * jnp.mean(e_two * n_hidden, axis=-1, keepdims=True)
    )
    hidden_low = jnp.concatenate(gather_tensor(hidden_grad.astype(BF)), axis=0)

    gu_weight_grad = dot_rows(n_all, gu_grad, BF)
    gu_block = ring_scatter(gu_weight_grad, 0)

    ffn_part = dot(active, down_full, BF)
    layer_quarter = (hidden + scatter_pair(ffn_part)).astype(BF)
    layer_output = absolute(gather_tensor(layer_quarter), BF)

    out_weight_grad = dot_rows(mixed_rel, hidden_low, BF)
    mixed_grad_rel = dot_cols(hidden_low, out_full, BF)
    mixed_grad = absolute(
        [mixed_grad_rel[j * quarter : (j + 1) * quarter] for j in range(tensor_size)], BF
    )
    query_grad, key_grad, value_grad = attend_backward(
        query_low,
        key_low,
        value_seq,
        log_total,
        mixed_grad.reshape(token_count, -1, HD),
        segment_row,
    )
    query_raw_grad = rotate(query_grad, cosine_wide, -sine_wide).astype(BF).reshape(token_count, -1)
    key_raw_grad = rotate(key_grad, cosine_wide, -sine_wide).astype(BF).reshape(token_count, -1)
    value_raw_grad = value_grad.astype(BF).reshape(token_count, -1)
    qkv_grad = jnp.concatenate([query_raw_grad, key_raw_grad, value_raw_grad], axis=1)
    e_one_part = dot_cols(relative(qkv_grad), qkv_full, BF)
    e_one = scatter_tensor(e_one_part)
    n_one = tokens_quarter * my_quarter(token_root)
    tokens_grad_quarter = hidden_grad + my_quarter(token_root) * (
        e_one - n_one * jnp.mean(e_one * n_one, axis=-1, keepdims=True)
    )
    tokens_grad = absolute(gather_tensor(tokens_grad_quarter.astype(BF)), F32)
    qkv_weight_grad = dot_rows(normed, qkv_grad, BF)

    def split_y(grad, axis, size):
        shape = grad.shape
        cut = grad.reshape(shape[:axis] + (groups, 2, size) + shape[axis + 1 :])
        mine = lax.dynamic_index_in_dim(cut, y_index, axis + 1, keepdims=False)
        other = lax.dynamic_index_in_dim(cut, 1 - y_index, axis + 1, keepdims=False)
        flat = shape[:axis] + (groups * size,) + shape[axis + 1 :]
        return mine.reshape(flat), other.reshape(flat)

    def scatter_whole(grad, axis, size):
        mine, other = split_y(grad, axis, size)
        got = swap_y(other)
        return ring_scatter((mine.astype(F32) + got.astype(F32)).astype(BF), axis)

    out_grad = scatter_whole(out_weight_grad, 1, output_weight.shape[1]).astype(F32)
    qkv_block = scatter_whole(qkv_weight_grad, 0, rows).astype(F32)

    def trade(block, axis_cut):
        mine = my_half(block, axis_cut, True)
        got = swap_y(my_half(block, axis_cut, False))
        return mine.astype(F32), got.astype(F32)

    def by_y(mine, got, axis):
        return jnp.where(
            y_index == 0,
            jnp.concatenate([mine, got], axis=axis),
            jnp.concatenate([got, mine], axis=axis),
        )

    gu_mine_rows, gu_got_rows = trade(gu_block, 0)
    gate_g = by_y(gu_mine_rows[:, :hidden_units], gu_got_rows[:, :hidden_units], 1)
    up_g = by_y(gu_mine_rows[:, hidden_units:], gu_got_rows[:, hidden_units:], 1)
    down_mine, down_got_cols = trade(down_block, 1)
    down_weight_grad = by_y(down_mine, down_got_cols, 0)

    attn_gain_part = jnp.sum(
        qkv_block * jnp.concatenate([query_weight, key_weight, value_weight], axis=1).astype(F32),
        axis=1,
    )
    ffn_gain_part = jnp.sum(
        gate_g * gate_weight.astype(F32) + up_g * up_weight.astype(F32), axis=1
    )
    gain_grads = lax.psum(jnp.stack([attn_gain_part, ffn_gain_part]), "tensor")
    qkv_out = qkv_block * attn_scale
    return (
        layer_output,
        tokens_grad,
        gain_grads[0],
        qkv_out[:, :q_cols],
        qkv_out[:, q_cols : q_cols + kv_cols],
        qkv_out[:, q_cols + kv_cols :],
        out_grad,
        gain_grads[1],
        gate_g * ffn_scale,
        up_g * ffn_scale,
        down_weight_grad,
    )


def solution(mesh):
    return jax.shard_map(
        partial(shards, mesh.shape["dp"], mesh.shape["tensor"]),
        mesh=mesh,
        in_specs=(
            P("dp", None),
            P("dp", None),
            P("dp"),
            P("dp", "tensor"),
            P("dp", "tensor"),
            P("dp", "tensor"),
            P("tensor", "dp"),
            P("dp"),
            P("dp", "tensor"),
            P("dp", "tensor"),
            P("tensor", "dp"),
            P("dp", None),
        ),
        out_specs=(
            P("dp", None),
            P("dp", None),
            P("dp"),
            P("dp", "tensor"),
            P("dp", "tensor"),
            P("dp", "tensor"),
            P("tensor", "dp"),
            P("dp"),
            P("dp", "tensor"),
            P("dp", "tensor"),
            P("tensor", "dp"),
        ),
        check_vma=False,
    )
```

```python
from functools import partial
import math

import jax
import jax.numpy as jnp
from jax import lax
from jax.sharding import PartitionSpec as P

HD = 64
GROUP = 4
epsilon = 1e-05
BF = jnp.bfloat16
F32 = jnp.float32


def rope_tables(segment_row, head_size):
    length = segment_row.shape[0]
    places = jnp.arange(length, dtype=jnp.int32)
    boundary = jnp.concatenate([jnp.ones((1,), dtype=bool), segment_row[1:] != segment_row[:-1]])
    starts = lax.cummax(jnp.where(boundary, places, 0), axis=0)
    position = (places - starts).astype(jnp.float32)
    half_size = head_size // 2
    exponent = jnp.arange(half_size, dtype=jnp.float32) * 2.0 / head_size
    inverse = 1.0 / 500000.0**exponent
    wavelen = 2.0 * math.pi / inverse
    smooth = (8192.0 / wavelen - 1.0) / 3.0
    scaled = jnp.where(
        wavelen < 2048.0,
        inverse,
        jnp.where(
            wavelen > 8192.0, inverse / 32.0, (1.0 - smooth) * inverse / 32.0 + smooth * inverse
        ),
    )
    angles = position[:, None] * scaled[None, :]
    cosine_table = jnp.cos(angles)
    sine_table = jnp.sin(angles)
    return (
        jnp.concatenate([cosine_table, cosine_table], axis=-1),
        jnp.concatenate([sine_table, sine_table], axis=-1),
    )


def rotate(values, cosine_table, sine_table):
    half_size = values.shape[-1] // 2
    turned = jnp.concatenate([-values[..., half_size:], values[..., :half_size]], axis=-1)
    return values * cosine_table + turned * sine_table


def dot_rows(left, right, out=F32):
    return lax.dot_general(
        left, right, (((0,), (0,)), ((), ())), preferred_element_type=F32
    ).astype(out)


def dot_cols(left, right, out=F32):
    return lax.dot_general(
        left, right, (((1,), (1,)), ((), ())), preferred_element_type=F32
    ).astype(out)


def dot(left, right, out=F32):
    return jnp.dot(left, right, preferred_element_type=F32).astype(out)


def tie(value, *others):
    return lax.optimization_barrier((value, *others))[0]


def inverse_root(values):
    return lax.rsqrt(jnp.mean(values * values, axis=-1, keepdims=True) + epsilon)


def spans(length):
    rows = length // 4
    most = length // 2
    for start in range(0, length, rows):
        first = max(0, start - most + 1) // rows * rows
        yield start, rows, first, start + rows


def block_scores(query_block, key_block, segment_row, start, first):
    rows, keys = query_block.shape[0], key_block.shape[0]
    scores = jnp.einsum("qkgd,skd->kgqs", query_block, key_block, preferred_element_type=F32)
    row_ids = start + jnp.arange(rows, dtype=jnp.int32)
    col_ids = first + jnp.arange(keys, dtype=jnp.int32)
    same_doc = segment_row[start : start + rows][:, None] == segment_row[first : first + keys][None, :]
    allowed = same_doc & (col_ids[None, :] <= row_ids[:, None])
    return jnp.where(allowed, scores, -1000000000.0)


def attend_forward(query_seq, key_seq, value_seq, segment_row):
    length, kv_local, head_size = key_seq.shape
    grouped = query_seq.reshape(length, kv_local, -1, head_size)
    mixed_parts = []
    total_parts = []
    for start, rows, first, last in spans(length):
        scores = block_scores(
            grouped[start : start + rows], key_seq[first:last], segment_row, start, first
        )
        row_max = jnp.max(scores, axis=-1, keepdims=True)
        log_total = jnp.log(jnp.sum(jnp.exp(scores - row_max), axis=-1, keepdims=True)) + row_max
        soft_low = jnp.exp(scores - log_total).astype(BF)
        mixed_block = jnp.einsum(
            "kgqs,skd->qkgd", soft_low, value_seq[first:last], preferred_element_type=F32
        )
        mixed_parts.append(mixed_block.reshape(rows, -1).astype(BF))
        total_parts.append(log_total)
    return (jnp.concatenate(mixed_parts, axis=0), total_parts)


def attend_backward(query_seq, key_seq, value_seq, total_parts, grad_seq, segment_row):
    length, kv_local, head_size = key_seq.shape
    grouped = query_seq.reshape(length, kv_local, -1, head_size)
    grad_grouped = grad_seq.reshape(length, kv_local, -1, head_size)
    score_scale = head_size ** (-0.5)
    query_parts = []
    key_grad = jnp.zeros(key_seq.shape, F32)
    value_grad = jnp.zeros(value_seq.shape, F32)
    for (start, rows, first, last), log_total in zip(spans(length), total_parts):
        query_block = grouped[start : start + rows]
        grad_block = grad_grouped[start : start + rows]
        key_block, value_block = key_seq[first:last], value_seq[first:last]
        scores = block_scores(query_block, key_block, segment_row, start, first)
        soft_weights = jnp.exp(scores - log_total)
        soft_grad = jnp.einsum("qkgd,skd->kgqs", grad_block, value_block, preferred_element_type=F32)
        score_grad = (
            soft_weights * (soft_grad - jnp.sum(soft_weights * soft_grad, axis=-1, keepdims=True))
        ).astype(BF)
        query_parts.append(
            jnp.einsum("kgqs,skd->qkgd", score_grad, key_block, preferred_element_type=F32)
            * score_scale
        )
        key_grad = key_grad.at[first:last].add(
            jnp.einsum("kgqs,qkgd->skd", score_grad, query_block, preferred_element_type=F32)
        )
        value_grad = value_grad.at[first:last].add(
            jnp.einsum(
                "kgqs,qkgd->skd", soft_weights.astype(BF), grad_block, preferred_element_type=F32
            )
        )
    query_grad = jnp.concatenate(query_parts, axis=0).reshape(length, -1, head_size)
    return (query_grad, key_grad, value_grad)


def shards(
    dp_size,
    tensor_size,
    tokens,
    segment_ids,
    attn_gain,
    query_weight,
    key_weight,
    value_weight,
    output_weight,
    ffn_gain,
    gate_weight,
    up_weight,
    down_weight,
    cotangent,
):
    groups = dp_size // 2
    dp_index = lax.axis_index("dp")
    z_index, y_index = dp_index // 2, dp_index % 2
    t_index = lax.axis_index("tensor")
    token_count, width = tokens.shape
    rows = query_weight.shape[0]
    quarter = token_count // tensor_size
    half_quarter = quarter // 2

    def swap_y(value):
        return lax.ppermute(value, "dp", [(i, i ^ 1) for i in range(dp_size)])

    def swap_x(value):
        return lax.ppermute(value, "tensor", [(i, i ^ 2) for i in range(tensor_size)])

    def swap_core(value):
        return lax.ppermute(value, "tensor", [(i, i ^ 1) for i in range(tensor_size)])

    def hop(value):
        return lax.ppermute(value, "dp", [(i, (i + 2) % dp_size) for i in range(dp_size)])

    def ring_gather(value):
        pieces = [value]
        for _ in range(groups - 1):
            pieces.append(hop(pieces[-1]))
        return pieces

    def place(pieces, side, axis):
        size = pieces[0][0].shape[axis]
        shape = list(pieces[0][0].shape)
        shape[axis] = size * dp_size
        whole = jnp.zeros(shape, BF)
        for value, step, y_of in pieces:
            block = ((z_index - step) % groups) * 2 + y_of
            start = [0, 0]
            start[axis] = block * size
            whole = lax.dynamic_update_slice(whole, value, tuple(start))
        return whole

    def my_half(value, axis, mine):
        size = value.shape[axis] // 2
        which = y_index if mine else 1 - y_index
        return lax.dynamic_slice_in_dim(value, which * size, size, axis)

    def relative(value):
        return jnp.concatenate(
            [
                lax.dynamic_slice_in_dim(value, (t_index ^ j) * quarter, quarter, 0)
                for j in range(tensor_size)
            ],
            axis=0,
        )

    def absolute(pieces, dtype):
        whole = jnp.zeros((quarter * tensor_size, pieces[0].shape[1]), dtype)
        for j, piece in enumerate(pieces):
            whole = lax.dynamic_update_slice(
                whole, piece.astype(dtype), ((t_index ^ j) * quarter, 0)
            )
        return whole

    attn_scale = attn_gain.astype(F32)[:, None]
    ffn_scale = ffn_gain.astype(F32)[:, None]

    def scaled(weight, scale):
        return (weight.astype(F32) * scale).astype(BF)

    qkv_local = scaled(jnp.concatenate([query_weight, key_weight, value_weight], axis=1), attn_scale)
    qkv_ring = ring_gather(qkv_local)
    qkv_other = [swap_y(v) for v in qkv_ring]
    qkv_full = place(
        [(v, s, y_index) for s, v in enumerate(qkv_ring)]
        + [(v, s, 1 - y_index) for s, v in enumerate(qkv_other)],
        None,
        0,
    )
    out_ring = ring_gather(tie(output_weight, qkv_ring[-2]))
    out_other = [swap_y(v) for v in out_ring]
    out_full = place(
        [(v, s, y_index) for s, v in enumerate(out_ring)]
        + [(v, s, 1 - y_index) for s, v in enumerate(out_other)],
        None,
        1,
    )

    z_groups = [[i for i in range(dp_size) if i % 2 == side] for side in range(2)]

    def gather_z(value):
        return lax.all_gather(value, "dp", axis_index_groups=z_groups, axis=0, tiled=True)

    def scatter_z(value):
        return lax.psum_scatter(
            value, "dp", axis_index_groups=z_groups, scatter_dimension=0, tiled=True
        )

    def by_y(mine, got, axis):
        return jnp.where(
            y_index == 0,
            jnp.concatenate([mine, got], axis=axis),
            jnp.concatenate([got, mine], axis=axis),
        )

    gate_scaled, up_scaled = scaled(gate_weight, ffn_scale), scaled(up_weight, ffn_scale)
    gu_mine = jnp.concatenate([my_half(gate_scaled, 1, True), my_half(up_scaled, 1, True)], axis=1)
    gu_send = jnp.concatenate([my_half(gate_scaled, 1, False), my_half(up_scaled, 1, False)], axis=1)
    gu_got = swap_y(gu_send)
    gu_full = gather_z(tie(by_y(gu_mine, gu_got, 0), qkv_ring[-1]))
    down_t = down_weight.T
    down_got = swap_y(tie(my_half(down_t, 1, False), gu_got))
    down_full = gather_z(tie(by_y(my_half(down_t, 1, True), down_got, 0), gu_full))
    cot_rel = relative(cotangent)
    cot_y = swap_y(tie(cot_rel[:quarter], down_got))
    cot_yx = swap_x(cot_y)
    cot_yc = swap_core(jnp.concatenate([cot_y, cot_yx], axis=0))
    cot_all = jnp.concatenate(
        [cot_rel, cot_y, cot_yc[:quarter], cot_yx, cot_yc[quarter:]], axis=0
    )

    tokens_float = tokens.astype(F32)
    token_root = inverse_root(tokens_float)
    normed = (tokens_float * token_root).astype(BF)
    qkv_raw = dot(normed, qkv_full)
    q_cols, kv_cols = query_weight.shape[1], key_weight.shape[1]
    segment_row = segment_ids[0]
    cosine_table, sine_table = rope_tables(segment_row, HD)
    cosine_wide, sine_wide = cosine_table[:, None, :], sine_table[:, None, :]
    query_raw = qkv_raw[:, :q_cols].reshape(token_count, -1, HD)
    key_raw = qkv_raw[:, q_cols : q_cols + kv_cols].reshape(token_count, -1, HD)
    value_seq = qkv_raw[:, q_cols + kv_cols :].astype(BF).reshape(token_count, -1, HD)
    query_low = (rotate(query_raw, cosine_wide, sine_wide) * HD ** (-0.5)).astype(BF)
    key_low = rotate(key_raw, cosine_wide, sine_wide).astype(BF)
    mixed, log_total = attend_forward(query_low, key_low, value_seq, segment_row)
    mixed_rel = relative(mixed)
    attn_part = dot(mixed_rel, out_full, BF)

    def two_way(first, second):
        return first.astype(F32) + second.astype(F32)

    def scatter_tensor(part):
        send = jnp.concatenate([part[quarter : 2 * quarter], part[3 * quarter :]], axis=0)
        got = swap_core(send)
        keep = two_way(part[:quarter], got[:quarter])
        pass_on = two_way(part[2 * quarter : 3 * quarter], got[quarter:]).astype(BF)
        return keep + swap_x(pass_on).astype(F32)

    def gather_tensor(piece):
        from_core = swap_core(piece)
        from_x = swap_x(piece)
        from_both = swap_core(from_x)
        return [piece, from_core, from_x, from_both]

    def my_quarter(value):
        return lax.dynamic_slice_in_dim(value, t_index * quarter, quarter, 0)

    tokens_quarter = my_quarter(tokens).astype(F32)
    hidden = tokens_quarter + scatter_tensor(attn_part)
    hidden_root = inverse_root(hidden)
    n_two = (hidden * hidden_root).astype(BF)

    first, second = n_two[:half_quarter], n_two[half_quarter:]
    first_x, second_y = swap_x(first), swap_y(second)
    first_y = swap_y(jnp.concatenate([first, first_x], axis=0))
    second_x = swap_x(jnp.concatenate([second, second_y], axis=0))
    held = jnp.concatenate(
        [
            first,
            second,
            first_x,
            second_x[:half_quarter],
            first_y[:half_quarter],
            second_y,
            first_y[half_quarter:],
            second_x[half_quarter:],
        ],
        axis=0,
    )
    crossed = swap_core(held)
    n_all = jnp.concatenate(
        [
            piece
            for y_side in range(2)
            for x_side in range(2)
            for piece in (
                held[(2 * y_side + x_side) * quarter : (2 * y_side + x_side + 1) * quarter],
                crossed[(2 * y_side + x_side) * quarter : (2 * y_side + x_side + 1) * quarter],
            )
        ],
        axis=0,
    )
    hidden_units = gate_weight.shape[1] // 2
    gu_values = dot(n_all, gu_full, BF)
    gate_values = gu_values[:, :hidden_units].astype(F32)
    up_values = gu_values[:, hidden_units:].astype(F32)
    sig = jax.nn.sigmoid(gate_values)
    silu = gate_values * sig
    active = (silu * up_values).astype(BF)

    def scatter_pair(part):
        blocks = [part[j * quarter : (j + 1) * quarter] for j in range(8)]
        got = swap_core(jnp.concatenate([blocks[1], blocks[3], blocks[5], blocks[7]], axis=0))
        kept = [
            two_way(blocks[2 * j], got[j * quarter : (j + 1) * quarter]) for j in range(4)
        ]
        top = [v[:half_quarter] for v in kept]
        low = [v[half_quarter:] for v in kept]
        top_got = swap_x(jnp.concatenate([top[1], top[3]], axis=0).astype(BF)).astype(F32)
        low_got = swap_y(jnp.concatenate([low[2], low[3]], axis=0).astype(BF)).astype(F32)
        top_keep = top[0] + top_got[:half_quarter]
        top_pass = (top[2] + top_got[half_quarter:]).astype(BF)
        low_keep = low[0] + low_got[:half_quarter]
        low_pass = (low[1] + low_got[half_quarter:]).astype(BF)
        return jnp.concatenate(
            [
                top_keep + swap_y(top_pass).astype(F32),
                low_keep + swap_x(low_pass).astype(F32),
            ],
            axis=0,
        )

    down_grad = dot_rows(cot_all, active, BF)
    down_block = scatter_z(down_grad)

    active_grad = dot(cot_all, down_full)
    gate_grad = (active_grad * up_values * (sig * (1.0 + gate_values * (1.0 - sig)))).astype(BF)
    up_grad = (active_grad * silu).astype(BF)
    gu_grad = jnp.concatenate([gate_grad, up_grad], axis=1)
    e_part = dot_cols(gu_grad, gu_full, BF)
    e_two = scatter_pair(e_part)
    n_hidden = hidden * hidden_root
    cot_quarter = my_quarter(cotangent).astype(F32)
    hidden_grad = cot_quarter + hidden_root * (
        e_two - n_hidden * jnp.mean(e_two * n_hidden, axis=-1, keepdims=True)
    )
    hidden_low = jnp.concatenate(gather_tensor(hidden_grad.astype(BF)), axis=0)

    gu_weight_grad = dot_rows(n_all, gu_grad, BF)
    gu_block = scatter_z(tie(gu_weight_grad, down_block))

    ffn_part = dot_cols(active, down_full, BF)
    layer_quarter = (hidden + scatter_pair(ffn_part)).astype(BF)
    layer_output = absolute(gather_tensor(layer_quarter), BF)

    out_weight_grad = dot_rows(hidden_low, mixed_rel, BF)
    mixed_grad_rel = dot_cols(hidden_low, out_full, BF)
    mixed_grad = absolute(
        [mixed_grad_rel[j * quarter : (j + 1) * quarter] for j in range(tensor_size)], BF
    )
    query_grad, key_grad, value_grad = attend_backward(
        query_low,
        key_low,
        value_seq,
        log_total,
        mixed_grad.reshape(token_count, -1, HD),
        segment_row,
    )
    query_raw_grad = rotate(query_grad, cosine_wide, -sine_wide).astype(BF).reshape(token_count, -1)
    key_raw_grad = rotate(key_grad, cosine_wide, -sine_wide).astype(BF).reshape(token_count, -1)
    value_raw_grad = value_grad.astype(BF).reshape(token_count, -1)
    qkv_grad = jnp.concatenate([query_raw_grad, key_raw_grad, value_raw_grad], axis=1)
    e_one_part = dot_cols(relative(qkv_grad), qkv_full, BF)
    e_one = scatter_tensor(e_one_part)
    n_one = tokens_quarter * my_quarter(token_root)
    tokens_grad_quarter = hidden_grad + my_quarter(token_root) * (
        e_one - n_one * jnp.mean(e_one * n_one, axis=-1, keepdims=True)
    )
    tokens_grad = absolute(gather_tensor(tokens_grad_quarter.astype(BF)), F32)
    qkv_weight_grad = dot_rows(normed, qkv_grad, BF)

    def scatter_whole(grad, size):
        cut = grad.reshape(groups, 2, size, -1)
        mine = lax.dynamic_index_in_dim(cut, y_index, 1, keepdims=False)
        other = lax.dynamic_index_in_dim(cut, 1 - y_index, 1, keepdims=False)
        got = swap_y(other.reshape(groups * size, -1))
        both = (mine.reshape(groups * size, -1).astype(F32) + got.astype(F32)).astype(BF)
        return scatter_z(both).astype(F32)

    out_grad = scatter_whole(out_weight_grad, output_weight.shape[1]).T
    qkv_block = scatter_whole(qkv_weight_grad, rows)

    def trade(block, axis_cut):
        mine = my_half(block, axis_cut, True)
        got = swap_y(my_half(block, axis_cut, False))
        return mine.astype(F32), got.astype(F32)

    gu_mine_rows, gu_got_rows = trade(gu_block, 0)
    gate_g = by_y(gu_mine_rows[:, :hidden_units], gu_got_rows[:, :hidden_units], 1)
    up_g = by_y(gu_mine_rows[:, hidden_units:], gu_got_rows[:, hidden_units:], 1)
    down_weight_grad = by_y(*trade(down_block, 0), 1).T

    attn_gain_part = jnp.sum(
        qkv_block * jnp.concatenate([query_weight, key_weight, value_weight], axis=1).astype(F32),
        axis=1,
    )
    ffn_gain_part = jnp.sum(
        gate_g * gate_weight.astype(F32) + up_g * up_weight.astype(F32), axis=1
    )

    def sum_tensor(value):
        value = value + swap_core(value)
        return value + swap_x(value)

    attn_gain_grad, ffn_gain_grad = sum_tensor(attn_gain_part), sum_tensor(ffn_gain_part)
    qkv_out = qkv_block * attn_scale
    return (
        layer_output,
        tokens_grad,
        attn_gain_grad,
        qkv_out[:, :q_cols],
        qkv_out[:, q_cols : q_cols + kv_cols],
        qkv_out[:, q_cols + kv_cols :],
        out_grad,
        ffn_gain_grad,
        gate_g * ffn_scale,
        up_g * ffn_scale,
        down_weight_grad,
    )


def solution(mesh):
    return jax.shard_map(
        partial(shards, mesh.shape["dp"], mesh.shape["tensor"]),
        mesh=mesh,
        in_specs=(
            P("dp", None),
            P("dp", None),
            P("dp"),
            P("dp", "tensor"),
            P("dp", "tensor"),
            P("dp", "tensor"),
            P("tensor", "dp"),
            P("dp"),
            P("dp", "tensor"),
            P("dp", "tensor"),
            P("tensor", "dp"),
            P("dp", None),
        ),
        out_specs=(
            P("dp", None),
            P("dp", None),
            P("dp"),
            P("dp", "tensor"),
            P("dp", "tensor"),
            P("dp", "tensor"),
            P("tensor", "dp"),
            P("dp"),
            P("dp", "tensor"),
            P("dp", "tensor"),
            P("tensor", "dp"),
        ),
        check_vma=False,
    )
```

```python
from functools import partial
import math

import jax
import jax.numpy as jnp
from jax import lax
from jax.sharding import PartitionSpec as P

HD = 64
GROUP = 4
epsilon = 1e-05
BF = jnp.bfloat16
F32 = jnp.float32


def rope_tables(segment_row, head_size):
    length = segment_row.shape[0]
    places = jnp.arange(length, dtype=jnp.int32)
    boundary = jnp.concatenate([jnp.ones((1,), dtype=bool), segment_row[1:] != segment_row[:-1]])
    starts = lax.cummax(jnp.where(boundary, places, 0), axis=0)
    position = (places - starts).astype(jnp.float32)
    half_size = head_size // 2
    exponent = jnp.arange(half_size, dtype=jnp.float32) * 2.0 / head_size
    inverse = 1.0 / 500000.0**exponent
    wavelen = 2.0 * math.pi / inverse
    smooth = (8192.0 / wavelen - 1.0) / 3.0
    scaled = jnp.where(
        wavelen < 2048.0,
        inverse,
        jnp.where(
            wavelen > 8192.0, inverse / 32.0, (1.0 - smooth) * inverse / 32.0 + smooth * inverse
        ),
    )
    angles = position[:, None] * scaled[None, :]
    cosine_table = jnp.cos(angles)
    sine_table = jnp.sin(angles)
    return (
        jnp.concatenate([cosine_table, cosine_table], axis=-1),
        jnp.concatenate([sine_table, sine_table], axis=-1),
    )


def rotate(values, cosine_table, sine_table):
    half_size = values.shape[-1] // 2
    turned = jnp.concatenate([-values[..., half_size:], values[..., :half_size]], axis=-1)
    return values * cosine_table + turned * sine_table


def dot_rows(left, right, out=F32):
    return lax.dot_general(
        left, right, (((0,), (0,)), ((), ())), preferred_element_type=F32
    ).astype(out)


def dot_cols(left, right, out=F32):
    return lax.dot_general(
        left, right, (((1,), (1,)), ((), ())), preferred_element_type=F32
    ).astype(out)


def dot(left, right, out=F32):
    return jnp.dot(left, right, preferred_element_type=F32).astype(out)


def tie(value, *others):
    return lax.optimization_barrier((value, *others))[0]


def inverse_root(values):
    return lax.rsqrt(jnp.mean(values * values, axis=-1, keepdims=True) + epsilon)


def spans(length):
    rows = length // 4
    most = length // 2
    for start in range(0, length, rows):
        first = max(0, start - most + 1) // rows * rows
        yield start, rows, first, start + rows


def block_scores(query_block, key_block, segment_row, start, first):
    rows, keys = query_block.shape[0], key_block.shape[0]
    scores = jnp.einsum("qkgd,skd->kgqs", query_block, key_block, preferred_element_type=F32)
    row_ids = start + jnp.arange(rows, dtype=jnp.int32)
    col_ids = first + jnp.arange(keys, dtype=jnp.int32)
    same_doc = segment_row[start : start + rows][:, None] == segment_row[first : first + keys][None, :]
    allowed = same_doc & (col_ids[None, :] <= row_ids[:, None])
    return jnp.where(allowed, scores, -1000000000.0)


def attend_forward(query_seq, key_seq, value_seq, segment_row, gates):
    length, kv_local, head_size = key_seq.shape
    grouped = query_seq.reshape(length, kv_local, -1, head_size)
    mixed_parts = []
    total_parts = []
    for (start, rows, first, last), gate in zip(spans(length), gates):
        query_block = grouped[start : start + rows]
        if gate:
            query_block = tie(query_block, *gate)
        scores = block_scores(query_block, key_seq[first:last], segment_row, start, first)
        row_max = jnp.max(scores, axis=-1, keepdims=True)
        log_total = jnp.log(jnp.sum(jnp.exp(scores - row_max), axis=-1, keepdims=True)) + row_max
        soft_low = jnp.exp(scores - log_total).astype(BF)
        mixed_block = jnp.einsum(
            "kgqs,skd->qkgd", soft_low, value_seq[first:last], preferred_element_type=F32
        )
        mixed_parts.append(mixed_block.reshape(rows, -1).astype(BF))
        total_parts.append(log_total)
    return (jnp.concatenate(mixed_parts, axis=0), total_parts)


def attend_backward(query_seq, key_seq, value_seq, total_parts, grad_seq, segment_row, gates):
    length, kv_local, head_size = key_seq.shape
    grouped = query_seq.reshape(length, kv_local, -1, head_size)
    grad_grouped = grad_seq.reshape(length, kv_local, -1, head_size)
    score_scale = head_size ** (-0.5)
    query_parts = []
    key_grad = jnp.zeros(key_seq.shape, F32)
    value_grad = jnp.zeros(value_seq.shape, F32)
    for (start, rows, first, last), log_total, gate in zip(spans(length), total_parts, gates):
        query_block = grouped[start : start + rows]
        grad_block = grad_grouped[start : start + rows]
        if gate:
            grad_block = tie(grad_block, *gate)
        key_block, value_block = key_seq[first:last], value_seq[first:last]
        scores = block_scores(query_block, key_block, segment_row, start, first)
        soft_weights = jnp.exp(scores - log_total)
        soft_grad = jnp.einsum("qkgd,skd->kgqs", grad_block, value_block, preferred_element_type=F32)
        score_grad = (
            soft_weights * (soft_grad - jnp.sum(soft_weights * soft_grad, axis=-1, keepdims=True))
        ).astype(BF)
        query_parts.append(
            jnp.einsum("kgqs,skd->qkgd", score_grad, key_block, preferred_element_type=F32)
            * score_scale
        )
        key_grad = key_grad.at[first:last].add(
            jnp.einsum("kgqs,qkgd->skd", score_grad, query_block, preferred_element_type=F32)
        )
        value_grad = value_grad.at[first:last].add(
            jnp.einsum(
                "kgqs,qkgd->skd", soft_weights.astype(BF), grad_block, preferred_element_type=F32
            )
        )
    query_grad = jnp.concatenate(query_parts, axis=0).reshape(length, -1, head_size)
    return (query_grad, key_grad, value_grad)


def shards(
    dp_size,
    tensor_size,
    tokens,
    segment_ids,
    attn_gain,
    query_weight,
    key_weight,
    value_weight,
    output_weight,
    ffn_gain,
    gate_weight,
    up_weight,
    down_weight,
    cotangent,
):
    groups = dp_size // 2
    dp_index = lax.axis_index("dp")
    z_index, y_index = dp_index // 2, dp_index % 2
    t_index = lax.axis_index("tensor")
    token_count, width = tokens.shape
    rows = query_weight.shape[0]
    quarter = token_count // tensor_size
    half_quarter = quarter // 2

    def swap_y(value):
        return lax.ppermute(value, "dp", [(i, i ^ 1) for i in range(dp_size)])

    def swap_x(value):
        return lax.ppermute(value, "tensor", [(i, i ^ 2) for i in range(tensor_size)])

    def swap_core(value):
        return lax.ppermute(value, "tensor", [(i, i ^ 1) for i in range(tensor_size)])

    def hop(value):
        return lax.ppermute(value, "dp", [(i, (i + 2) % dp_size) for i in range(dp_size)])

    def ring_gather(value):
        pieces = [value]
        for _ in range(groups - 1):
            pieces.append(hop(pieces[-1]))
        return pieces

    def place(pieces, side, axis):
        size = pieces[0][0].shape[axis]
        shape = list(pieces[0][0].shape)
        shape[axis] = size * dp_size
        whole = jnp.zeros(shape, BF)
        for value, step, y_of in pieces:
            block = ((z_index - step) % groups) * 2 + y_of
            start = [0, 0]
            start[axis] = block * size
            whole = lax.dynamic_update_slice(whole, value, tuple(start))
        return whole

    def my_half(value, axis, mine):
        size = value.shape[axis] // 2
        which = y_index if mine else 1 - y_index
        return lax.dynamic_slice_in_dim(value, which * size, size, axis)

    def relative(value):
        return jnp.concatenate(
            [
                lax.dynamic_slice_in_dim(value, (t_index ^ j) * quarter, quarter, 0)
                for j in range(tensor_size)
            ],
            axis=0,
        )

    def absolute(pieces, dtype):
        whole = jnp.zeros((quarter * tensor_size, pieces[0].shape[1]), dtype)
        for j, piece in enumerate(pieces):
            whole = lax.dynamic_update_slice(
                whole, piece.astype(dtype), ((t_index ^ j) * quarter, 0)
            )
        return whole

    attn_scale = attn_gain.astype(F32)[:, None]
    ffn_scale = ffn_gain.astype(F32)[:, None]

    def scaled(weight, scale):
        return (weight.astype(F32) * scale).astype(BF)

    gate_scaled, up_scaled = scaled(gate_weight, ffn_scale), scaled(up_weight, ffn_scale)
    gu_send = jnp.concatenate([my_half(gate_scaled, 1, False), my_half(up_scaled, 1, False)], axis=1)
    gu_got = swap_y(gu_send)
    qkv_local = scaled(jnp.concatenate([query_weight, key_weight, value_weight], axis=1), attn_scale)
    qkv_local = tie(qkv_local, gu_send)
    qkv_ring = ring_gather(qkv_local)
    qkv_other = [swap_y(v) for v in qkv_ring]
    qkv_full = place(
        [(v, s, y_index) for s, v in enumerate(qkv_ring)]
        + [(v, s, 1 - y_index) for s, v in enumerate(qkv_other)],
        None,
        0,
    )
    out_ring = ring_gather(tie(output_weight, qkv_ring[-2]))
    out_other = [swap_y(v) for v in out_ring]
    out_full = place(
        [(v, s, y_index) for s, v in enumerate(out_ring)]
        + [(v, s, 1 - y_index) for s, v in enumerate(out_other)],
        None,
        1,
    )

    z_groups = [[i for i in range(dp_size) if i % 2 == side] for side in range(2)]

    def gather_z(value):
        return lax.all_gather(value, "dp", axis_index_groups=z_groups, axis=0, tiled=True)

    def scatter_z(value):
        return lax.psum_scatter(
            value, "dp", axis_index_groups=z_groups, scatter_dimension=0, tiled=True
        )

    def by_y(mine, got, axis):
        return jnp.where(
            y_index == 0,
            jnp.concatenate([mine, got], axis=axis),
            jnp.concatenate([got, mine], axis=axis),
        )

    def pair_rows(mine, got):
        size = mine.shape[0]
        whole = jnp.zeros((2 * size, mine.shape[1]), BF)
        whole = lax.dynamic_update_slice(whole, mine, (y_index * size, 0))
        return lax.dynamic_update_slice(whole, got, ((1 - y_index) * size, 0))

    gu_mine = jnp.concatenate([my_half(gate_scaled, 1, True), my_half(up_scaled, 1, True)], axis=1)
    gu_pair = pair_rows(gu_mine, gu_got)
    gu_full = gather_z(tie(gu_pair, qkv_ring[-1]))
    down_t = down_weight.T
    down_got = swap_y(tie(my_half(down_t, 1, False), out_other[-1]))
    down_pair = pair_rows(my_half(down_t, 1, True), down_got)
    down_full = gather_z(tie(down_pair, gu_pair))
    cot_rel = relative(cotangent)
    cot_y = swap_y(tie(cot_rel[:quarter], down_got))
    cot_yx = swap_x(cot_y)
    cot_yc = swap_core(jnp.concatenate([cot_y, cot_yx], axis=0))
    cot_all = jnp.concatenate(
        [cot_rel, cot_y, cot_yc[:quarter], cot_yx, cot_yc[quarter:]], axis=0
    )

    tokens_float = tokens.astype(F32)
    token_root = inverse_root(tokens_float)
    normed = (tokens_float * token_root).astype(BF)
    qkv_raw = dot(tie(normed, gu_pair), qkv_full)
    q_cols, kv_cols = query_weight.shape[1], key_weight.shape[1]
    segment_row = segment_ids[0]
    cosine_table, sine_table = rope_tables(segment_row, HD)
    cosine_wide, sine_wide = cosine_table[:, None, :], sine_table[:, None, :]
    query_raw = qkv_raw[:, :q_cols].reshape(token_count, -1, HD)
    key_raw = qkv_raw[:, q_cols : q_cols + kv_cols].reshape(token_count, -1, HD)
    value_seq = qkv_raw[:, q_cols + kv_cols :].astype(BF).reshape(token_count, -1, HD)
    query_low = (rotate(query_raw, cosine_wide, sine_wide) * HD ** (-0.5)).astype(BF)
    key_low = rotate(key_raw, cosine_wide, sine_wide).astype(BF)
    out_gates = ((), (out_ring[1],), (out_ring[2],), (out_ring[3], out_other[1]))
    mixed, log_total = attend_forward(query_low, key_low, value_seq, segment_row, out_gates)
    mixed_rel = relative(mixed)
    attn_part = dot(tie(mixed_rel, down_pair), out_full, BF)

    def two_way(first, second):
        return first.astype(F32) + second.astype(F32)

    def scatter_tensor(part):
        send = jnp.concatenate([part[quarter : 2 * quarter], part[3 * quarter :]], axis=0)
        got = swap_core(send)
        keep = two_way(part[:quarter], got[:quarter])
        pass_on = two_way(part[2 * quarter : 3 * quarter], got[quarter:]).astype(BF)
        return keep + swap_x(pass_on).astype(F32)

    def gather_tensor(piece):
        from_core = swap_core(piece)
        from_x = swap_x(piece)
        from_both = swap_core(from_x)
        return [piece, from_core, from_x, from_both]

    def my_quarter(value):
        return lax.dynamic_slice_in_dim(value, t_index * quarter, quarter, 0)

    tokens_quarter = my_quarter(tokens).astype(F32)
    hidden = tokens_quarter + scatter_tensor(attn_part)
    hidden_root = inverse_root(hidden)
    n_two = (hidden * hidden_root).astype(BF)

    first, second = n_two[:half_quarter], n_two[half_quarter:]
    first_x, second_y = swap_x(first), swap_y(second)
    first_y = swap_y(jnp.concatenate([first, first_x], axis=0))
    second_x = swap_x(jnp.concatenate([second, second_y], axis=0))
    held = jnp.concatenate(
        [
            first,
            second,
            first_x,
            second_x[:half_quarter],
            first_y[:half_quarter],
            second_y,
            first_y[half_quarter:],
            second_x[half_quarter:],
        ],
        axis=0,
    )
    crossed = swap_core(held)
    n_all = jnp.concatenate(
        [
            piece
            for y_side in range(2)
            for x_side in range(2)
            for piece in (
                held[(2 * y_side + x_side) * quarter : (2 * y_side + x_side + 1) * quarter],
                crossed[(2 * y_side + x_side) * quarter : (2 * y_side + x_side + 1) * quarter],
            )
        ],
        axis=0,
    )
    hidden_units = gate_weight.shape[1] // 2
    gu_values = dot(n_all, gu_full, BF)
    gate_values = gu_values[:, :hidden_units].astype(F32)
    up_values = gu_values[:, hidden_units:].astype(F32)
    sig = jax.nn.sigmoid(gate_values)
    silu = gate_values * sig
    active = (silu * up_values).astype(BF)

    def pair_core(part):
        return swap_core(
            jnp.concatenate([part[j * quarter : (j + 1) * quarter] for j in (1, 3, 5, 7)], axis=0)
        )

    def pair_kept(part, got):
        kept = [
            two_way(
                part[2 * j * quarter : (2 * j + 1) * quarter], got[j * quarter : (j + 1) * quarter]
            )
            for j in range(4)
        ]
        top = [v[:half_quarter] for v in kept]
        low = [v[half_quarter:] for v in kept]
        sends = (
            jnp.concatenate([top[1], top[3]], axis=0).astype(BF),
            jnp.concatenate([low[2], low[3]], axis=0).astype(BF),
        )
        return top, low, sends

    def pair_pass(top, low, sends):
        top_got = swap_x(sends[0]).astype(F32)
        low_got = swap_y(sends[1]).astype(F32)
        top_keep = top[0] + top_got[:half_quarter]
        top_pass = (top[2] + top_got[half_quarter:]).astype(BF)
        low_keep = low[0] + low_got[:half_quarter]
        low_pass = (low[1] + low_got[half_quarter:]).astype(BF)
        return top_keep, low_keep, (top_pass, low_pass)

    def pair_sum(top_keep, low_keep, passes):
        return jnp.concatenate(
            [
                top_keep + swap_y(passes[0]).astype(F32),
                low_keep + swap_x(passes[1]).astype(F32),
            ],
            axis=0,
        )

    def ring_begin(block):
        return hop(block(1))

    def ring_step(received, block, step):
        return hop((received.astype(F32) + block(step + 1)).astype(BF))

    def ring_end(received, block):
        return received.astype(F32) + block(groups)

    def z_block(grad):
        size = grad.shape[0] // groups

        def block(back):
            return lax.dynamic_slice_in_dim(
                grad, (z_index - back) % groups * size, size, 0
            )

        return block

    down_grad = dot_rows(cot_all, active, BF)
    down_part = z_block(down_grad)
    down_runs = [ring_begin(down_part)]
    for step in range(1, groups - 1):
        down_runs.append(ring_step(down_runs[-1], down_part, step))
    down_block = ring_end(down_runs[-1], down_part).astype(BF)

    active_grad = dot(tie(cot_all, down_grad), down_full)
    gate_grad = (active_grad * up_values * (sig * (1.0 + gate_values * (1.0 - sig)))).astype(BF)
    up_grad = (active_grad * silu).astype(BF)
    gu_grad = jnp.concatenate([gate_grad, up_grad], axis=1)
    e_part = dot_cols(tie(gu_grad, down_runs[0]), gu_full, BF)
    e_got = pair_core(e_part)
    gate_weight_grad = dot_rows(n_all, tie(gu_grad[:, :hidden_units], e_part, down_runs[1]), BF)
    gate_block = scatter_z(gate_weight_grad)
    e_kept = pair_kept(tie(e_part, gate_weight_grad), e_got)
    up_weight_grad = dot_rows(n_all, tie(gu_grad[:, hidden_units:], *e_kept[2]), BF)
    up_block = scatter_z(up_weight_grad)
    ffn_part = dot_cols(tie(active, up_weight_grad, down_runs[-1]), down_full, BF)
    ffn_got = pair_core(ffn_part)
    e_top, e_low, e_sends = e_kept
    e_top[2] = tie(e_top[2], ffn_part)
    e_two = pair_sum(*pair_pass(e_top, e_low, e_sends))
    n_hidden = hidden * hidden_root
    cot_quarter = my_quarter(cotangent).astype(F32)
    hidden_grad = cot_quarter + hidden_root * (
        e_two - n_hidden * jnp.mean(e_two * n_hidden, axis=-1, keepdims=True)
    )
    hidden_low = jnp.concatenate(gather_tensor(hidden_grad.astype(BF)), axis=0)

    ffn_kept = pair_kept(ffn_part, ffn_got)
    ffn_sends = tuple(tie(v, hidden_low) for v in ffn_kept[2])
    ffn_passed = pair_pass(ffn_kept[0], ffn_kept[1], ffn_sends)
    layer_quarter = (hidden + pair_sum(*ffn_passed)).astype(BF)
    layer_output = absolute(gather_tensor(layer_quarter), BF)

    mixed_grad_rel = dot_cols(hidden_low, out_full, BF)
    out_weight_grad = dot_rows(hidden_low, tie(mixed_rel, mixed_grad_rel), BF)
    def y_parts(grad):
        cut = grad.reshape(groups, 2, grad.shape[0] // (2 * groups), -1)

        def pick(back, side):
            start = ((z_index - back) % groups, side, 0, 0)
            return lax.dynamic_slice(cut, start, (1, 1) + cut.shape[2:])[0, 0]

        return lambda back: pick(back, y_index), lambda back: pick(back, 1 - y_index)

    def with_other(mine, other):
        return lambda back: mine(back).astype(F32) + other[back - 1].astype(F32)

    out_mine, out_other_y = y_parts(out_weight_grad)
    out_sent = swap_y(jnp.stack([out_other_y(back) for back in range(1, groups + 1)]))
    out_part = with_other(out_mine, out_sent)
    out_runs = [hop(out_part(1).astype(BF))]
    for step in range(1, groups - 1):
        out_runs.append(ring_step(out_runs[-1], out_part, step))
    out_grad = ring_end(out_runs[-1], out_part).T

    mixed_grad = absolute(
        [mixed_grad_rel[j * quarter : (j + 1) * quarter] for j in range(tensor_size)], BF
    )
    query_grad, key_grad, value_grad = attend_backward(
        query_low,
        key_low,
        value_seq,
        log_total,
        mixed_grad.reshape(token_count, -1, HD),
        segment_row,
        (
            ffn_sends + (out_weight_grad,),
            (out_sent,),
            ffn_passed[2] + (out_runs[0],),
            (layer_quarter, out_runs[1]),
        ),
    )
    query_raw_grad = rotate(query_grad, cosine_wide, -sine_wide).astype(BF).reshape(token_count, -1)
    key_raw_grad = rotate(key_grad, cosine_wide, -sine_wide).astype(BF).reshape(token_count, -1)
    value_raw_grad = value_grad.astype(BF).reshape(token_count, -1)
    qkv_grad = jnp.concatenate([query_raw_grad, key_raw_grad, value_raw_grad], axis=1)
    qkv_weight_grad = dot_rows(normed, qkv_grad, BF)
    e_one_part = dot_cols(relative(tie(qkv_grad, qkv_weight_grad)), qkv_full, BF)
    e_one = scatter_tensor(e_one_part)
    n_one = tokens_quarter * my_quarter(token_root)
    tokens_grad_quarter = hidden_grad + my_quarter(token_root) * (
        e_one - n_one * jnp.mean(e_one * n_one, axis=-1, keepdims=True)
    )
    tokens_grad = absolute(gather_tensor(tokens_grad_quarter.astype(BF)), F32)

    qkv_mine, qkv_other_y = y_parts(qkv_weight_grad)
    qkv_sent = [swap_y(qkv_other_y(back)) for back in range(1, groups + 1)]
    qkv_part = with_other(qkv_mine, qkv_sent)
    qkv_run = hop(qkv_part(1).astype(BF))
    for step in range(1, groups - 1):
        qkv_run = ring_step(qkv_run, qkv_part, step)
    qkv_block = ring_end(qkv_run, qkv_part)

    def trade(block, axis_cut):
        mine = my_half(block, axis_cut, True)
        got = swap_y(my_half(block, axis_cut, False))
        return mine.astype(F32), got.astype(F32)

    gate_g = by_y(*trade(gate_block, 0), 1)
    up_g = by_y(*trade(up_block, 0), 1)
    down_weight_grad = by_y(*trade(down_block, 0), 1).T

    attn_gain_part = jnp.sum(
        qkv_block * jnp.concatenate([query_weight, key_weight, value_weight], axis=1).astype(F32),
        axis=1,
    )
    ffn_gain_part = jnp.sum(
        gate_g * gate_weight.astype(F32) + up_g * up_weight.astype(F32), axis=1
    )

    def sum_tensor(value):
        value = value + swap_core(value)
        return value + swap_x(value)

    attn_gain_grad, ffn_gain_grad = sum_tensor(attn_gain_part), sum_tensor(ffn_gain_part)
    qkv_out = qkv_block * attn_scale
    return (
        layer_output,
        tokens_grad,
        attn_gain_grad,
        qkv_out[:, :q_cols],
        qkv_out[:, q_cols : q_cols + kv_cols],
        qkv_out[:, q_cols + kv_cols :],
        out_grad,
        ffn_gain_grad,
        gate_g * ffn_scale,
        up_g * ffn_scale,
        down_weight_grad,
    )


def solution(mesh):
    return jax.shard_map(
        partial(shards, mesh.shape["dp"], mesh.shape["tensor"]),
        mesh=mesh,
        in_specs=(
            P("dp", None),
            P("dp", None),
            P("dp"),
            P("dp", "tensor"),
            P("dp", "tensor"),
            P("dp", "tensor"),
            P("tensor", "dp"),
            P("dp"),
            P("dp", "tensor"),
            P("dp", "tensor"),
            P("tensor", "dp"),
            P("dp", None),
        ),
        out_specs=(
            P("dp", None),
            P("dp", None),
            P("dp"),
            P("dp", "tensor"),
            P("dp", "tensor"),
            P("dp", "tensor"),
            P("tensor", "dp"),
            P("dp"),
            P("dp", "tensor"),
            P("dp", "tensor"),
            P("tensor", "dp"),
        ),
        check_vma=False,
    )
```

```python
from functools import partial
import math

import jax
import jax.numpy as jnp
from jax import lax
from jax.sharding import PartitionSpec as P

HD = 64
GROUP = 4
epsilon = 1e-05
BF = jnp.bfloat16
F32 = jnp.float32


def rope_tables(segment_row, head_size):
    length = segment_row.shape[0]
    places = jnp.arange(length, dtype=jnp.int32)
    boundary = jnp.concatenate([jnp.ones((1,), dtype=bool), segment_row[1:] != segment_row[:-1]])
    starts = lax.cummax(jnp.where(boundary, places, 0), axis=0)
    position = (places - starts).astype(jnp.float32)
    half_size = head_size // 2
    exponent = jnp.arange(half_size, dtype=jnp.float32) * 2.0 / head_size
    inverse = 1.0 / 500000.0**exponent
    wavelen = 2.0 * math.pi / inverse
    smooth = (8192.0 / wavelen - 1.0) / 3.0
    scaled = jnp.where(
        wavelen < 2048.0,
        inverse,
        jnp.where(
            wavelen > 8192.0, inverse / 32.0, (1.0 - smooth) * inverse / 32.0 + smooth * inverse
        ),
    )
    angles = position[:, None] * scaled[None, :]
    cosine_table = jnp.cos(angles)
    sine_table = jnp.sin(angles)
    return (
        jnp.concatenate([cosine_table, cosine_table], axis=-1),
        jnp.concatenate([sine_table, sine_table], axis=-1),
    )


def rotate(values, cosine_table, sine_table):
    half_size = values.shape[-1] // 2
    turned = jnp.concatenate([-values[..., half_size:], values[..., :half_size]], axis=-1)
    return values * cosine_table + turned * sine_table


def dot_rows(left, right, out=F32):
    return lax.dot_general(
        left, right, (((0,), (0,)), ((), ())), preferred_element_type=F32
    ).astype(out)


def dot_cols(left, right, out=F32):
    return lax.dot_general(
        left, right, (((1,), (1,)), ((), ())), preferred_element_type=F32
    ).astype(out)


def dot(left, right, out=F32):
    return jnp.dot(left, right, preferred_element_type=F32).astype(out)


def tie(value, *others):
    return lax.optimization_barrier((value, *others))[0]


def inverse_root(values):
    return lax.rsqrt(jnp.mean(values * values, axis=-1, keepdims=True) + epsilon)


def spans(length):
    rows = length // 4
    most = length // 2
    for start in range(0, length, rows):
        first = max(0, start - most + 1) // rows * rows
        yield start, rows, first, start + rows


def block_scores(query_block, key_block, segment_row, start, first):
    rows, keys = query_block.shape[0], key_block.shape[0]
    scores = jnp.einsum("qkgd,skd->kgqs", query_block, key_block, preferred_element_type=F32)
    row_ids = start + jnp.arange(rows, dtype=jnp.int32)
    col_ids = first + jnp.arange(keys, dtype=jnp.int32)
    same_doc = segment_row[start : start + rows][:, None] == segment_row[first : first + keys][None, :]
    allowed = same_doc & (col_ids[None, :] <= row_ids[:, None])
    return jnp.where(allowed, scores, -1000000000.0)


def attend_forward(query_seq, key_seq, value_seq, segment_row):
    length, kv_local, head_size = key_seq.shape
    grouped = query_seq.reshape(length, kv_local, -1, head_size)
    mixed_parts = []
    total_parts = []
    for start, rows, first, last in spans(length):
        query_block = grouped[start : start + rows]
        scores = block_scores(query_block, key_seq[first:last], segment_row, start, first)
        row_max = jnp.max(scores, axis=-1, keepdims=True)
        log_total = jnp.log(jnp.sum(jnp.exp(scores - row_max), axis=-1, keepdims=True)) + row_max
        soft_low = jnp.exp(scores - log_total).astype(BF)
        mixed_block = jnp.einsum(
            "kgqs,skd->qkgd", soft_low, value_seq[first:last], preferred_element_type=F32
        )
        mixed_parts.append(mixed_block.reshape(rows, -1).astype(BF))
        total_parts.append(log_total)
    return (jnp.concatenate(mixed_parts, axis=0), total_parts)


def block_backward(query_block, key_block, value_block, log_total, grad_block, segment_row, start, first):
    scores = block_scores(query_block, key_block, segment_row, start, first)
    soft_weights = jnp.exp(scores - log_total)
    soft_grad = jnp.einsum("qkgd,skd->kgqs", grad_block, value_block, preferred_element_type=F32)
    score_grad = (
        soft_weights * (soft_grad - jnp.sum(soft_weights * soft_grad, axis=-1, keepdims=True))
    ).astype(BF)
    query_part = jnp.einsum("kgqs,skd->qkgd", score_grad, key_block, preferred_element_type=F32)
    key_part = jnp.einsum("kgqs,qkgd->skd", score_grad, query_block, preferred_element_type=F32)
    value_part = jnp.einsum(
        "kgqs,qkgd->skd", soft_weights.astype(BF), grad_block, preferred_element_type=F32
    )
    return query_part * query_block.shape[-1] ** (-0.5), key_part, value_part


def shards(
    dp_size,
    tensor_size,
    tokens,
    segment_ids,
    attn_gain,
    query_weight,
    key_weight,
    value_weight,
    output_weight,
    ffn_gain,
    gate_weight,
    up_weight,
    down_weight,
    cotangent,
):
    groups = dp_size // 2
    dp_index = lax.axis_index("dp")
    z_index, y_index = dp_index // 2, dp_index % 2
    t_index = lax.axis_index("tensor")
    token_count, width = tokens.shape
    rows = query_weight.shape[0]
    quarter = token_count // tensor_size
    half_quarter = quarter // 2

    def swap_y(value):
        return lax.ppermute(value, "dp", [(i, i ^ 1) for i in range(dp_size)])

    def swap_x(value):
        return lax.ppermute(value, "tensor", [(i, i ^ 2) for i in range(tensor_size)])

    def swap_core(value):
        return lax.ppermute(value, "tensor", [(i, i ^ 1) for i in range(tensor_size)])

    def hop(value):
        return lax.ppermute(value, "dp", [(i, (i + 2) % dp_size) for i in range(dp_size)])

    def my_half(value, axis, mine):
        size = value.shape[axis] // 2
        which = y_index if mine else 1 - y_index
        return lax.dynamic_slice_in_dim(value, which * size, size, axis)

    def relative(value):
        return jnp.concatenate(
            [
                lax.dynamic_slice_in_dim(value, (t_index ^ j) * quarter, quarter, 0)
                for j in range(tensor_size)
            ],
            axis=0,
        )

    def absolute(pieces, dtype):
        whole = jnp.zeros((quarter * tensor_size, pieces[0].shape[1]), dtype)
        for j, piece in enumerate(pieces):
            whole = lax.dynamic_update_slice(
                whole, piece.astype(dtype), ((t_index ^ j) * quarter, 0)
            )
        return whole

    z_groups = [[i for i in range(dp_size) if i % 2 == side] for side in range(2)]

    def gather_z(value):
        return lax.all_gather(value, "dp", axis_index_groups=z_groups, axis=0, tiled=True)

    def scatter_z(value):
        return lax.psum_scatter(
            value, "dp", axis_index_groups=z_groups, scatter_dimension=0, tiled=True
        )

    def by_y(mine, got, axis):
        return jnp.where(
            y_index == 0,
            jnp.concatenate([mine, got], axis=axis),
            jnp.concatenate([got, mine], axis=axis),
        )

    def pair_rows(mine, got):
        size = mine.shape[0]
        whole = jnp.zeros((2 * size, mine.shape[1]), BF)
        whole = lax.dynamic_update_slice(whole, mine, (y_index * size, 0))
        return lax.dynamic_update_slice(whole, got, ((1 - y_index) * size, 0))

    def interleave(mine, other):
        mine = mine.reshape(groups, 1, rows, -1)
        other = other.reshape(groups, 1, rows, -1)
        return by_y(mine, other, 1).reshape(2 * groups * rows, -1)

    attn_scale = attn_gain.astype(F32)[:, None]
    ffn_scale = ffn_gain.astype(F32)[:, None]

    def scaled(weight, scale):
        return (weight.astype(F32) * scale).astype(BF)

    q_cols, kv_cols = query_weight.shape[1], key_weight.shape[1]
    qkv_cols = q_cols + 2 * kv_cols
    hidden_units = gate_weight.shape[1] // 2
    first_units = hidden_units * 3 // 8
    part_units = (first_units, hidden_units - first_units)
    trio = (scaled(gate_weight, ffn_scale), scaled(up_weight, ffn_scale), down_weight.T)

    def trio_part(side, part):
        start = side * hidden_units + part * first_units
        return jnp.concatenate(
            [lax.dynamic_slice_in_dim(weight, start, part_units[part], 1) for weight in trio], axis=1
        )

    attn_local = jnp.concatenate(
        [
            scaled(jnp.concatenate([query_weight, key_weight, value_weight], axis=1), attn_scale),
            output_weight.T,
        ],
        axis=1,
    )
    attn_z = gather_z(attn_local)
    send_a = tie(trio_part(1 - y_index, 0), attn_local)
    got_a = swap_y(send_a)
    got_b = swap_y(tie(trio_part(1 - y_index, 1), got_a))
    pair_a = pair_rows(trio_part(y_index, 0), got_a)
    pair_b = pair_rows(trio_part(y_index, 1), got_b)
    full_a = gather_z(tie(pair_a, attn_local))
    full_b = gather_z(tie(pair_b, pair_a))
    qkv_z, out_z = attn_z[:, :qkv_cols], attn_z[:, qkv_cols:]
    qkv_other = swap_y(tie(qkv_z, pair_b))
    out_other = swap_y(tie(out_z, qkv_other))
    qkv_full = interleave(qkv_z, qkv_other)
    out_full = interleave(out_z, out_other)

    tokens_float = tokens.astype(F32)
    token_root = inverse_root(tokens_float)
    normed = (tokens_float * token_root).astype(BF)
    qkv_raw = dot(normed, qkv_full)
    segment_row = segment_ids[0]
    cosine_table, sine_table = rope_tables(segment_row, HD)
    cosine_wide, sine_wide = cosine_table[:, None, :], sine_table[:, None, :]
    query_raw = qkv_raw[:, :q_cols].reshape(token_count, -1, HD)
    key_raw = qkv_raw[:, q_cols : q_cols + kv_cols].reshape(token_count, -1, HD)
    value_seq = qkv_raw[:, q_cols + kv_cols :].astype(BF).reshape(token_count, -1, HD)
    query_low = (rotate(query_raw, cosine_wide, sine_wide) * HD ** (-0.5)).astype(BF)
    key_low = rotate(key_raw, cosine_wide, sine_wide).astype(BF)
    mixed, log_total = attend_forward(query_low, key_low, value_seq, segment_row)
    mixed_rel = relative(mixed)
    attn_part = dot_cols(mixed_rel, out_full, BF)

    def two_way(first, second):
        return first.astype(F32) + second.astype(F32)

    def scatter_tensor(part):
        send = jnp.concatenate([part[quarter : 2 * quarter], part[3 * quarter :]], axis=0)
        got = swap_core(send)
        keep = two_way(part[:quarter], got[:quarter])
        pass_on = two_way(part[2 * quarter : 3 * quarter], got[quarter:]).astype(BF)
        return keep + swap_x(pass_on).astype(F32)

    def gather_tensor(piece):
        from_core = swap_core(piece)
        from_x = swap_x(piece)
        from_both = swap_core(from_x)
        return [piece, from_core, from_x, from_both]

    def my_quarter(value):
        return lax.dynamic_slice_in_dim(value, t_index * quarter, quarter, 0)

    tokens_quarter = my_quarter(tokens).astype(F32)
    hidden = tokens_quarter + scatter_tensor(attn_part)
    hidden_root = inverse_root(hidden)
    n_two = (hidden * hidden_root).astype(BF)

    first, second = n_two[:half_quarter], n_two[half_quarter:]
    top = jnp.concatenate([first, swap_x(first)], axis=0)
    low = jnp.concatenate([second, swap_y(second)], axis=0)
    top, low = lax.optimization_barrier((top, low))
    n_held = jnp.concatenate([top, swap_y(top), low, swap_x(low)], axis=0)
    n_held = tie(n_held, full_a)
    n_all = jnp.concatenate([n_held, swap_core(n_held)], axis=0)

    def quarter_of(value, other):
        return lax.dynamic_slice_in_dim(value, (t_index ^ other) * quarter, quarter, 0)

    cot_own, cot_x = quarter_of(cotangent, 0), quarter_of(cotangent, 2)
    cot_y = swap_y(tie(cot_own, n_held))
    cot_yx = swap_x(cot_y)
    cot_held = jnp.concatenate(
        [v[:half_quarter] for v in (cot_own, cot_x, cot_y, cot_yx)]
        + [v[half_quarter:] for v in (cot_own, cot_y, cot_x, cot_yx)],
        axis=0,
    )
    cot_all = jnp.concatenate([cot_held, swap_core(cot_held)], axis=0)

    side_rows = 4 * quarter

    def pair_sends(part, got):
        def kept(start):
            return two_way(part[start : start + quarter], got[start : start + quarter])

        keeps = (kept(0), kept(2 * quarter))
        return keeps, (kept(quarter).astype(BF), kept(3 * quarter).astype(BF))

    def pair_pass(keeps, sends):
        top_sum = keeps[0] + swap_y(sends[0]).astype(F32)
        low_sum = keeps[1] + swap_x(sends[1]).astype(F32)
        passes = (top_sum[half_quarter:].astype(BF), low_sum[half_quarter:].astype(BF))
        return (top_sum[:half_quarter], low_sum[:half_quarter]), passes

    def pair_sum(keeps, passes):
        return jnp.concatenate(
            [keeps[0] + swap_x(passes[0]).astype(F32), keeps[1] + swap_y(passes[1]).astype(F32)],
            axis=0,
        )

    def units(full, rows_all):
        count = full.shape[1] // 3
        gu = dot(rows_all, full[:, : 2 * count], BF)
        gate_values = gu[:, :count].astype(F32)
        up_values = gu[:, count:].astype(F32)
        sig = jax.nn.sigmoid(gate_values)
        silu = gate_values * sig
        return gate_values, up_values, sig, silu, (silu * up_values).astype(BF)

    def units_grad(full, parts, cot_rows):
        gate_values, up_values, sig, silu, _ = parts
        active_grad = dot(cot_rows, full[:, full.shape[1] // 3 * 2 :])
        gate_grad = active_grad * up_values * (sig * (1.0 + gate_values * (1.0 - sig)))
        return jnp.concatenate([gate_grad.astype(BF), (active_grad * silu).astype(BF)], axis=1)

    parts_a = units(full_a, n_all)
    active_a = parts_a[-1]
    down_grad_a = dot_rows(cot_all, active_a, BF)
    down_block_a = scatter_z(down_grad_a)
    gu_grad_a = units_grad(full_a, parts_a, tie(cot_all, down_grad_a))
    gu_weight_grad_a = dot_rows(n_all, gu_grad_a, BF)
    gu_block_a = scatter_z(gu_weight_grad_a)
    gu_a, gu_b = (v[:, : 2 * n] for v, n in zip((full_a, full_b), part_units))
    down_a, down_b = (v[:, 2 * n :] for v, n in zip((full_a, full_b), part_units))
    e_part_a = dot_cols(tie(gu_grad_a, gu_weight_grad_a), gu_a, BF)
    ffn_part_a = dot_cols(tie(active_a, e_part_a), down_a, BF)

    parts_b = units(full_b, tie(n_all, ffn_part_a))
    active_b = parts_b[-1]
    gu_grad_b = units_grad(full_b, parts_b, cot_all)
    own, other = slice(0, side_rows), slice(side_rows, 2 * side_rows)
    e_cross = (dot_cols(gu_grad_b[other], gu_b) + e_part_a[other].astype(F32)).astype(BF)
    e_got = swap_core(e_cross)
    e_part = dot_cols(tie(gu_grad_b, e_cross)[own], gu_b) + e_part_a[own].astype(F32)
    e_part = e_part.astype(BF)
    down_grad_b = dot_rows(cot_all, tie(active_b, e_part, down_block_a), BF)
    down_block_b = scatter_z(down_grad_b)
    e_keeps, e_sends = pair_sends(tie(e_part, e_cross), e_got)
    gu_weight_grad_b = dot_rows(n_all, tie(gu_grad_b, down_grad_b, *e_sends), BF)
    gu_block_b = scatter_z(gu_weight_grad_b)
    ffn_cross = dot_cols(tie(active_b, gu_weight_grad_b)[other], down_b)
    ffn_cross = (ffn_cross + ffn_part_a[other].astype(F32)).astype(BF)
    ffn_got = swap_core(ffn_cross)
    e_keeps, e_passes = pair_pass(tuple(tie(v, ffn_cross) for v in e_keeps), e_sends)
    ffn_part = dot_cols(tie(active_b, *e_passes)[own], down_b)
    ffn_part = (ffn_part + ffn_part_a[own].astype(F32)).astype(BF)
    e_two = pair_sum(tuple(tie(v, ffn_part) for v in e_keeps), e_passes)
    n_hidden = hidden * hidden_root
    cot_quarter = my_quarter(cotangent).astype(F32)
    hidden_grad = cot_quarter + hidden_root * (
        e_two - n_hidden * jnp.mean(e_two * n_hidden, axis=-1, keepdims=True)
    )
    hidden_low = jnp.concatenate(gather_tensor(hidden_grad.astype(BF)), axis=0)

    ffn_keeps, ffn_sends = pair_sends(ffn_part, ffn_got)
    ffn_sends = tuple(tie(v, hidden_low) for v in ffn_sends)
    ffn_keeps, ffn_passes = pair_pass(ffn_keeps, ffn_sends)
    layer_quarter = (hidden + pair_sum(ffn_keeps, ffn_passes)).astype(BF)
    layer_output = absolute(gather_tensor(layer_quarter), BF)

    def ring_step(received, block, step):
        return hop((received.astype(F32) + block(step + 1)).astype(BF))

    def ring_end(received, block):
        return received.astype(F32) + block(groups)

    mixed_grad_rel = dot(hidden_low, out_full, BF)
    out_weight_grad = dot_rows(hidden_low, tie(mixed_rel, mixed_grad_rel), BF)
    cut = out_weight_grad.reshape(groups, 2, rows, -1)
    out_mine = lax.dynamic_index_in_dim(cut, y_index, 1, keepdims=False)
    out_sent = swap_y(lax.dynamic_index_in_dim(cut, 1 - y_index, 1, keepdims=False))
    out_both = two_way(out_mine, out_sent).astype(BF).reshape(groups * rows, -1)
    out_block = scatter_z(out_both)
    out_grad = out_block.astype(F32).T
    mixed_grad = absolute(
        [mixed_grad_rel[j * quarter : (j + 1) * quarter] for j in range(tensor_size)], BF
    )
    gates = (
        ffn_sends + (out_weight_grad,),
        (gu_block_a,),
        ffn_passes + (out_both,),
        (layer_quarter, down_block_b),
    )
    grouped = query_low.reshape(token_count, -1, GROUP, HD)
    grad_grouped = mixed_grad.reshape(token_count, -1, GROUP, HD)
    key_grad = jnp.zeros(key_low.shape, F32)
    value_grad = jnp.zeros(value_seq.shape, F32)
    core_index, half_rows = t_index % 2, token_count // 2
    qkv_grad_parts, e_one_parts, query_parts = [], [], []
    for number, ((start, size, first_key, last), log_part, gate) in enumerate(
        zip(reversed(list(spans(token_count))), reversed(log_total), gates)
    ):
        grad_block = tie(grad_grouped[start : start + size], *gate)
        if number == 2:
            grad_block = tie(grad_block, e_one_parts[0])
        query_part, key_part, value_part = block_backward(
            grouped[start : start + size],
            key_low[first_key:last],
            value_seq[first_key:last],
            log_part,
            grad_block,
            segment_row,
            start,
            first_key,
        )
        key_grad = key_grad.at[first_key:last].add(key_part)
        value_grad = value_grad.at[first_key:last].add(value_part)
        query_parts.insert(0, query_part)
        if number % 2 == 1:
            span = slice(start, start + half_rows)
            cosine_span, sine_span = cosine_wide[span], -sine_wide[span]
            query_grad = jnp.concatenate(query_parts, axis=0).reshape(half_rows, -1, HD)
            qkv_grad_part = jnp.concatenate(
                [
                    rotate(query_grad, cosine_span, sine_span).reshape(half_rows, -1),
                    rotate(key_grad[span], cosine_span, sine_span).reshape(half_rows, -1),
                    value_grad[span].reshape(half_rows, -1),
                ],
                axis=1,
            ).astype(BF)
            query_parts = []
            qkv_grad_parts.insert(0, qkv_grad_part)
            if number == 1:
                e_one_parts.append(dot_cols(qkv_grad_part, qkv_full, BF))
    qkv_weight_grad = dot_rows(normed, jnp.concatenate(qkv_grad_parts, axis=0), BF)
    e_one_parts.append(dot_cols(tie(qkv_grad_parts[0], qkv_weight_grad), qkv_full, BF))

    def tokens_rows(part, start):
        size = part.shape[0] // 2

        def mine(value, base):
            return lax.dynamic_slice_in_dim(value, base + core_index * size, size, 0)

        got = swap_core(lax.dynamic_slice_in_dim(part, (1 - core_index) * size, size, 0))
        chip_sum = two_way(mine(part, 0), got).astype(BF)
        e_one = two_way(chip_sum, swap_x(chip_sum))
        grad_rows = lax.dynamic_slice_in_dim(
            hidden_low, (t_index ^ (start // quarter + core_index)) * quarter, size, 0
        ).astype(F32)
        root = mine(token_root, start)
        n_one = mine(tokens, start).astype(F32) * root
        own = grad_rows + root * (e_one - n_one * jnp.mean(e_one * n_one, axis=-1, keepdims=True))
        own = own.astype(BF)
        other = swap_core(own)
        return jnp.where(
            core_index == 0,
            jnp.concatenate([own, other], axis=0),
            jnp.concatenate([other, own], axis=0),
        ).astype(F32)

    tokens_grad = jnp.concatenate(
        [tokens_rows(e_one_parts[1], 0), tokens_rows(e_one_parts[0], half_rows)], axis=0
    )

    qkv_cut = qkv_weight_grad.reshape(groups, 2, rows, -1)

    def qkv_pick(side):
        def pick(back):
            start = ((z_index - back) % groups, side, 0, 0)
            return lax.dynamic_slice(qkv_cut, start, (1, 1, rows, qkv_cols))[0, 0]

        return pick

    qkv_mine, qkv_other_y = qkv_pick(y_index), qkv_pick(1 - y_index)
    qkv_sent = [swap_y(qkv_other_y(back)) for back in range(1, groups + 1)]

    def qkv_part(back):
        return two_way(qkv_mine(back), qkv_sent[back - 1])

    qkv_run = hop(qkv_part(1).astype(BF))
    for step in range(1, groups - 1):
        qkv_run = ring_step(qkv_run, qkv_part, step)
    qkv_block = ring_end(qkv_run, qkv_part)

    def trade(block):
        mine = my_half(block, 0, True)
        return mine, swap_y(my_half(block, 0, False))

    traded = [
        [trade(tie(block, last)) for block, last in zip(pair, (layer_quarter, qkv_weight_grad))]
        for pair in ((gu_block_a, gu_block_b), (down_block_a, down_block_b))
    ]

    def all_units(pairs, place):
        def side(which):
            return jnp.concatenate(
                [pair[which][:, place * n : (place + 1) * n] for pair, n in zip(pairs, part_units)],
                axis=1,
            )

        return by_y(side(0), side(1), 1).astype(F32)

    gate_g, up_g = all_units(traded[0], 0), all_units(traded[0], 1)
    down_weight_grad = all_units(traded[1], 0).T

    attn_gain_part = jnp.sum(
        qkv_block * jnp.concatenate([query_weight, key_weight, value_weight], axis=1).astype(F32),
        axis=1,
    )
    ffn_gain_part = jnp.sum(
        gate_g * gate_weight.astype(F32) + up_g * up_weight.astype(F32), axis=1
    )

    def sum_tensor(value):
        value = value + swap_core(value)
        return value + swap_x(value)

    attn_gain_grad, ffn_gain_grad = sum_tensor(jnp.stack([attn_gain_part, ffn_gain_part]))
    qkv_out = qkv_block * attn_scale
    return (
        layer_output,
        tokens_grad,
        attn_gain_grad,
        qkv_out[:, :q_cols],
        qkv_out[:, q_cols : q_cols + kv_cols],
        qkv_out[:, q_cols + kv_cols :],
        out_grad,
        ffn_gain_grad,
        gate_g * ffn_scale,
        up_g * ffn_scale,
        down_weight_grad,
    )


def solution(mesh):
    return jax.shard_map(
        partial(shards, mesh.shape["dp"], mesh.shape["tensor"]),
        mesh=mesh,
        in_specs=(
            P("dp", None),
            P("dp", None),
            P("dp"),
            P("dp", "tensor"),
            P("dp", "tensor"),
            P("dp", "tensor"),
            P("tensor", "dp"),
            P("dp"),
            P("dp", "tensor"),
            P("dp", "tensor"),
            P("tensor", "dp"),
            P("dp", None),
        ),
        out_specs=(
            P("dp", None),
            P("dp", None),
            P("dp"),
            P("dp", "tensor"),
            P("dp", "tensor"),
            P("dp", "tensor"),
            P("tensor", "dp"),
            P("dp"),
            P("dp", "tensor"),
            P("dp", "tensor"),
            P("tensor", "dp"),
        ),
        check_vma=False,
    )
```

```python
from functools import partial
import math

import jax
import jax.numpy as jnp
from jax import lax
from jax.sharding import PartitionSpec as P

HD = 64
GROUP = 4
epsilon = 1e-05
BF = jnp.bfloat16
F32 = jnp.float32


def rope_tables(segment_row, head_size):
    length = segment_row.shape[0]
    places = jnp.arange(length, dtype=jnp.int32)
    boundary = jnp.concatenate([jnp.ones((1,), dtype=bool), segment_row[1:] != segment_row[:-1]])
    starts = lax.cummax(jnp.where(boundary, places, 0), axis=0)
    position = (places - starts).astype(jnp.float32)
    half_size = head_size // 2
    exponent = jnp.arange(half_size, dtype=jnp.float32) * 2.0 / head_size
    inverse = 1.0 / 500000.0**exponent
    wavelen = 2.0 * math.pi / inverse
    smooth = (8192.0 / wavelen - 1.0) / 3.0
    scaled = jnp.where(
        wavelen < 2048.0,
        inverse,
        jnp.where(
            wavelen > 8192.0, inverse / 32.0, (1.0 - smooth) * inverse / 32.0 + smooth * inverse
        ),
    )
    angles = position[:, None] * scaled[None, :]
    cosine_table = jnp.cos(angles)
    sine_table = jnp.sin(angles)
    return (
        jnp.concatenate([cosine_table, cosine_table], axis=-1),
        jnp.concatenate([sine_table, sine_table], axis=-1),
    )


def rotate(values, cosine_table, sine_table):
    half_size = values.shape[-1] // 2
    turned = jnp.concatenate([-values[..., half_size:], values[..., :half_size]], axis=-1)
    return values * cosine_table + turned * sine_table


def dot_rows(left, right, out=F32):
    return lax.dot_general(
        left, right, (((0,), (0,)), ((), ())), preferred_element_type=F32
    ).astype(out)


def dot_cols(left, right, out=F32):
    return lax.dot_general(
        left, right, (((1,), (1,)), ((), ())), preferred_element_type=F32
    ).astype(out)


def dot(left, right, out=F32):
    return jnp.dot(left, right, preferred_element_type=F32).astype(out)


def tie(value, *others):
    return lax.optimization_barrier((value, *others))[0]


def inverse_root(values):
    return lax.rsqrt(jnp.mean(values * values, axis=-1, keepdims=True) + epsilon)


def spans(length):
    rows = length // 4
    most = length // 2
    for start in range(0, length, rows):
        first = max(0, start - most + 1) // rows * rows
        yield start, rows, first, start + rows


def block_scores(query_block, key_block, segment_row, start, first):
    rows, keys = query_block.shape[0], key_block.shape[0]
    scores = jnp.einsum("qkgd,skd->kgqs", query_block, key_block, preferred_element_type=F32)
    row_ids = start + jnp.arange(rows, dtype=jnp.int32)
    col_ids = first + jnp.arange(keys, dtype=jnp.int32)
    same_doc = segment_row[start : start + rows][:, None] == segment_row[first : first + keys][None, :]
    allowed = same_doc & (col_ids[None, :] <= row_ids[:, None])
    return jnp.where(allowed, scores, -1000000000.0)


def attend_forward(query_seq, key_seq, value_seq, segment_row):
    length, kv_local, head_size = key_seq.shape
    grouped = query_seq.reshape(length, kv_local, -1, head_size)
    mixed_parts = []
    total_parts = []
    for start, rows, first, last in spans(length):
        query_block = grouped[start : start + rows]
        scores = block_scores(query_block, key_seq[first:last], segment_row, start, first)
        row_max = jnp.max(scores, axis=-1, keepdims=True)
        log_total = jnp.log(jnp.sum(jnp.exp(scores - row_max), axis=-1, keepdims=True)) + row_max
        soft_low = jnp.exp(scores - log_total).astype(BF)
        mixed_block = jnp.einsum(
            "kgqs,skd->qkgd", soft_low, value_seq[first:last], preferred_element_type=F32
        )
        mixed_parts.append(mixed_block.reshape(rows, -1).astype(BF))
        total_parts.append(log_total)
    return (jnp.concatenate(mixed_parts, axis=0), total_parts)


def block_backward(query_block, key_block, value_block, log_total, grad_block, segment_row, start, first):
    scores = block_scores(query_block, key_block, segment_row, start, first)
    soft_weights = jnp.exp(scores - log_total)
    soft_grad = jnp.einsum("qkgd,skd->kgqs", grad_block, value_block, preferred_element_type=F32)
    score_grad = (
        soft_weights * (soft_grad - jnp.sum(soft_weights * soft_grad, axis=-1, keepdims=True))
    ).astype(BF)
    query_part = jnp.einsum("kgqs,skd->qkgd", score_grad, key_block, preferred_element_type=F32)
    key_part = jnp.einsum("kgqs,qkgd->skd", score_grad, query_block, preferred_element_type=F32)
    value_part = jnp.einsum(
        "kgqs,qkgd->skd", soft_weights.astype(BF), grad_block, preferred_element_type=F32
    )
    return query_part * query_block.shape[-1] ** (-0.5), key_part, value_part


def shards(
    dp_size,
    tensor_size,
    tokens,
    segment_ids,
    attn_gain,
    query_weight,
    key_weight,
    value_weight,
    output_weight,
    ffn_gain,
    gate_weight,
    up_weight,
    down_weight,
    cotangent,
):
    groups = dp_size // 2
    dp_index = lax.axis_index("dp")
    z_index, y_index = dp_index // 2, dp_index % 2
    t_index = lax.axis_index("tensor")
    token_count, width = tokens.shape
    rows = query_weight.shape[0]
    quarter = token_count // tensor_size
    half_quarter = quarter // 2

    def swap_y(value):
        return lax.ppermute(value, "dp", [(i, i ^ 1) for i in range(dp_size)])

    def swap_x(value):
        return lax.ppermute(value, "tensor", [(i, i ^ 2) for i in range(tensor_size)])

    def swap_core(value):
        return lax.ppermute(value, "tensor", [(i, i ^ 1) for i in range(tensor_size)])

    def hop(value):
        return lax.ppermute(value, "dp", [(i, (i + 2) % dp_size) for i in range(dp_size)])

    def my_half(value, axis, mine):
        size = value.shape[axis] // 2
        which = y_index if mine else 1 - y_index
        return lax.dynamic_slice_in_dim(value, which * size, size, axis)

    def relative(value):
        return jnp.concatenate(
            [
                lax.dynamic_slice_in_dim(value, (t_index ^ j) * quarter, quarter, 0)
                for j in range(tensor_size)
            ],
            axis=0,
        )

    def absolute(pieces, dtype):
        whole = jnp.zeros((quarter * tensor_size, pieces[0].shape[1]), dtype)
        for j, piece in enumerate(pieces):
            whole = lax.dynamic_update_slice(
                whole, piece.astype(dtype), ((t_index ^ j) * quarter, 0)
            )
        return whole

    z_groups = [[i for i in range(dp_size) if i % 2 == side] for side in range(2)]

    def gather_z(value):
        return lax.all_gather(value, "dp", axis_index_groups=z_groups, axis=0, tiled=True)

    def scatter_z(value):
        return lax.psum_scatter(
            value, "dp", axis_index_groups=z_groups, scatter_dimension=0, tiled=True
        )

    def by_y(mine, got, axis):
        return jnp.where(
            y_index == 0,
            jnp.concatenate([mine, got], axis=axis),
            jnp.concatenate([got, mine], axis=axis),
        )

    def pair_rows(mine, got):
        size = mine.shape[0]
        whole = jnp.zeros((2 * size, mine.shape[1]), BF)
        whole = lax.dynamic_update_slice(whole, mine, (y_index * size, 0))
        return lax.dynamic_update_slice(whole, got, ((1 - y_index) * size, 0))

    def interleave(mine, other):
        mine = mine.reshape(groups, 1, rows, -1)
        other = other.reshape(groups, 1, rows, -1)
        return by_y(mine, other, 1).reshape(2 * groups * rows, -1)

    attn_scale = attn_gain.astype(F32)[:, None]
    ffn_scale = ffn_gain.astype(F32)[:, None]

    def scaled(weight, scale):
        return (weight.astype(F32) * scale).astype(BF)

    q_cols, kv_cols = query_weight.shape[1], key_weight.shape[1]
    qkv_cols = q_cols + 2 * kv_cols
    hidden_units = gate_weight.shape[1] // 2
    first_units = hidden_units * 3 // 8
    part_units = (first_units, hidden_units - first_units)
    trio = (scaled(gate_weight, ffn_scale), scaled(up_weight, ffn_scale), down_weight.T)

    def trio_part(side, part):
        start = side * hidden_units + part * first_units
        return jnp.concatenate(
            [lax.dynamic_slice_in_dim(weight, start, part_units[part], 1) for weight in trio], axis=1
        )

    attn_local = jnp.concatenate(
        [
            scaled(jnp.concatenate([query_weight, key_weight, value_weight], axis=1), attn_scale),
            output_weight.T,
        ],
        axis=1,
    )
    attn_z = gather_z(attn_local)
    send_a = tie(trio_part(1 - y_index, 0), attn_local)
    got_a = swap_y(send_a)
    pair_a = pair_rows(trio_part(y_index, 0), got_a)
    full_a = gather_z(tie(pair_a, attn_local))
    got_b = swap_y(tie(trio_part(1 - y_index, 1), got_a))
    pair_b = pair_rows(trio_part(y_index, 1), got_b)
    full_b = gather_z(tie(pair_b, pair_a))
    qkv_z, out_z = attn_z[:, :qkv_cols], attn_z[:, qkv_cols:]
    qkv_other = swap_y(tie(qkv_z, pair_b))
    out_other = swap_y(tie(out_z, qkv_other))
    qkv_full = interleave(qkv_z, qkv_other)
    out_full = interleave(out_z, out_other)

    def quarter_of(value, other):
        return lax.dynamic_slice_in_dim(value, (t_index ^ other) * quarter, quarter, 0)

    cot_own, cot_x = quarter_of(cotangent, 0), quarter_of(cotangent, 2)
    cot_pair = swap_y(tie(jnp.concatenate([cot_own, cot_x], axis=0), out_other))

    tokens_float = tokens.astype(F32)
    token_root = inverse_root(tokens_float)
    normed = (tokens_float * token_root).astype(BF)
    qkv_raw = dot(normed, qkv_full)
    segment_row = segment_ids[0]
    cosine_table, sine_table = rope_tables(segment_row, HD)
    cosine_wide, sine_wide = cosine_table[:, None, :], sine_table[:, None, :]
    query_raw = qkv_raw[:, :q_cols].reshape(token_count, -1, HD)
    key_raw = qkv_raw[:, q_cols : q_cols + kv_cols].reshape(token_count, -1, HD)
    value_seq = qkv_raw[:, q_cols + kv_cols :].astype(BF).reshape(token_count, -1, HD)
    query_low = (rotate(query_raw, cosine_wide, sine_wide) * HD ** (-0.5)).astype(BF)
    key_low = rotate(key_raw, cosine_wide, sine_wide).astype(BF)
    mixed, log_total = attend_forward(query_low, key_low, value_seq, segment_row)
    mixed_rel = relative(mixed)
    attn_part = dot_cols(mixed_rel, out_full, BF)

    def two_way(first, second):
        return first.astype(F32) + second.astype(F32)

    def scatter_tensor(part):
        send = jnp.concatenate([part[quarter : 2 * quarter], part[3 * quarter :]], axis=0)
        got = swap_core(send)
        keep = two_way(part[:quarter], got[:quarter])
        pass_on = two_way(part[2 * quarter : 3 * quarter], got[quarter:]).astype(BF)
        return keep + swap_x(pass_on).astype(F32)

    def gather_tensor(piece):
        from_core = swap_core(piece)
        from_x = swap_x(piece)
        from_both = swap_core(from_x)
        return [piece, from_core, from_x, from_both]

    def my_quarter(value):
        return lax.dynamic_slice_in_dim(value, t_index * quarter, quarter, 0)

    tokens_quarter = my_quarter(tokens).astype(F32)
    hidden = tokens_quarter + scatter_tensor(attn_part)
    hidden_root = inverse_root(hidden)
    n_two = (hidden * hidden_root).astype(BF)

    first, second = n_two[:half_quarter], n_two[half_quarter:]
    top = jnp.concatenate([first, swap_x(first)], axis=0)
    low = jnp.concatenate([second, swap_y(second)], axis=0)
    top, low = lax.optimization_barrier((top, low))
    n_held = jnp.concatenate([top, swap_y(top), low, swap_x(low)], axis=0)
    n_held = tie(n_held, full_a)
    n_all = jnp.concatenate([n_held, swap_core(n_held)], axis=0)

    cot_pair = tie(cot_pair, n_two)
    cot_y, cot_yx = cot_pair[:quarter], cot_pair[quarter:]
    cot_held = jnp.concatenate(
        [v[:half_quarter] for v in (cot_own, cot_x, cot_y, cot_yx)]
        + [v[half_quarter:] for v in (cot_own, cot_y, cot_x, cot_yx)],
        axis=0,
    )
    cot_all = jnp.concatenate([cot_held, swap_core(cot_held)], axis=0)


    side_rows = 4 * quarter

    def pair_sends(part, got):
        def kept(start):
            return two_way(part[start : start + quarter], got[start : start + quarter])

        keeps = (kept(0), kept(2 * quarter))
        return keeps, (kept(quarter).astype(BF), kept(3 * quarter).astype(BF))

    def pair_pass(keeps, sends):
        top_sum = keeps[0] + swap_y(sends[0]).astype(F32)
        low_sum = keeps[1] + swap_x(sends[1]).astype(F32)
        passes = (top_sum[half_quarter:].astype(BF), low_sum[half_quarter:].astype(BF))
        return (top_sum[:half_quarter], low_sum[:half_quarter]), passes

    def pair_sum(keeps, passes):
        return jnp.concatenate(
            [keeps[0] + swap_x(passes[0]).astype(F32), keeps[1] + swap_y(passes[1]).astype(F32)],
            axis=0,
        )

    def units(full, rows_all):
        count = full.shape[1] // 3
        gu = dot(rows_all, full[:, : 2 * count], BF)
        gate_values = gu[:, :count].astype(F32)
        up_values = gu[:, count:].astype(F32)
        sig = jax.nn.sigmoid(gate_values)
        silu = gate_values * sig
        return gate_values, up_values, sig, silu, (silu * up_values).astype(BF)

    def units_grad(full, parts, cot_rows):
        gate_values, up_values, sig, silu, _ = parts
        active_grad = dot(cot_rows, full[:, full.shape[1] // 3 * 2 :])
        gate_grad = active_grad * up_values * (sig * (1.0 + gate_values * (1.0 - sig)))
        return jnp.concatenate([gate_grad.astype(BF), (active_grad * silu).astype(BF)], axis=1)

    parts_a = units(full_a, n_all)
    active_a = parts_a[-1]
    down_grad_a = dot_rows(cot_all, active_a, BF)
    down_block_a = scatter_z(down_grad_a)
    gu_grad_a = units_grad(full_a, parts_a, tie(cot_all, down_grad_a))
    gu_weight_grad_a = dot_rows(n_all, gu_grad_a, BF)
    gu_block_a = scatter_z(gu_weight_grad_a)
    gu_a, gu_b = (v[:, : 2 * n] for v, n in zip((full_a, full_b), part_units))
    down_a, down_b = (v[:, 2 * n :] for v, n in zip((full_a, full_b), part_units))
    e_part_a = dot_cols(tie(gu_grad_a, gu_weight_grad_a), gu_a, BF)
    ffn_part_a = dot_cols(tie(active_a, e_part_a), down_a, BF)

    parts_b = units(full_b, tie(n_all, ffn_part_a))
    active_b = parts_b[-1]
    gu_grad_b = units_grad(full_b, parts_b, cot_all)
    own, other = slice(0, side_rows), slice(side_rows, 2 * side_rows)
    e_cross = (dot_cols(gu_grad_b[other], gu_b) + e_part_a[other].astype(F32)).astype(BF)
    e_got = swap_core(e_cross)
    e_part = dot_cols(tie(gu_grad_b, e_cross)[own], gu_b) + e_part_a[own].astype(F32)
    e_part = e_part.astype(BF)
    down_grad_b = dot_rows(cot_all, tie(active_b, e_part, down_block_a), BF)
    down_block_b = scatter_z(down_grad_b)
    e_keeps, e_sends = pair_sends(tie(e_part, e_cross), e_got)
    gu_weight_grad_b = dot_rows(n_all, tie(gu_grad_b, down_grad_b, *e_sends), BF)
    gu_block_b = scatter_z(gu_weight_grad_b)
    ffn_cross = dot_cols(tie(active_b, gu_weight_grad_b)[other], down_b)
    ffn_cross = (ffn_cross + ffn_part_a[other].astype(F32)).astype(BF)
    ffn_got = swap_core(ffn_cross)
    e_keeps, e_passes = pair_pass(tuple(tie(v, ffn_cross) for v in e_keeps), e_sends)
    ffn_part = dot_cols(tie(active_b, *e_passes)[own], down_b)
    ffn_part = (ffn_part + ffn_part_a[own].astype(F32)).astype(BF)
    e_two = pair_sum(tuple(tie(v, ffn_part) for v in e_keeps), e_passes)
    n_hidden = hidden * hidden_root
    cot_quarter = my_quarter(cotangent).astype(F32)
    hidden_grad = cot_quarter + hidden_root * (
        e_two - n_hidden * jnp.mean(e_two * n_hidden, axis=-1, keepdims=True)
    )
    hidden_low = jnp.concatenate(gather_tensor(hidden_grad.astype(BF)), axis=0)

    def pair_rows_of(part, got, blocks):
        return jnp.concatenate(
            [
                two_way(
                    part[i * half_quarter : (i + 1) * half_quarter],
                    got[i * half_quarter : (i + 1) * half_quarter],
                )
                for i in blocks
            ],
            axis=0,
        )

    ffn_send = pair_rows_of(ffn_part, ffn_got, (2, 5, 3, 7)).astype(BF)
    ffn_keep = pair_rows_of(ffn_part, ffn_got, (0, 4, 1, 6))
    hidden_low = tie(hidden_low, ffn_send)
    ffn_sum = ffn_keep + swap_y(ffn_send).astype(F32)
    ffn_pass = ffn_sum[quarter:].astype(BF)
    layer_quarter = (hidden + ffn_sum[:quarter] + swap_x(ffn_pass).astype(F32)).astype(BF)

    def ring_end(received, block):
        return received.astype(F32) + block(groups)

    mixed_grad_rel = dot(hidden_low, out_full, BF)
    out_weight_grad = dot_rows(hidden_low, tie(mixed_rel, mixed_grad_rel), BF)
    cut = out_weight_grad.reshape(groups, 2, rows, -1)
    out_mine = lax.dynamic_index_in_dim(cut, y_index, 1, keepdims=False)
    out_send = lax.dynamic_index_in_dim(cut, 1 - y_index, 1, keepdims=False)
    out_sent = swap_y(tie(out_send, ffn_pass))
    out_both = two_way(out_mine, out_sent).astype(BF).reshape(groups * rows, -1)
    out_block = scatter_z(tie(out_both, gu_block_b))
    out_grad = out_block.astype(F32).T
    mixed_grad = absolute(
        [mixed_grad_rel[j * quarter : (j + 1) * quarter] for j in range(tensor_size)], BF
    )
    def trade(block):
        return my_half(block, 0, True), swap_y(my_half(block, 0, False))

    gu_trade_a, down_trade_a = trade(gu_block_a), trade(down_block_a)
    down_trade_b, gu_trade_b = trade(tie(down_block_b, mixed_grad_rel)), trade(gu_block_b)
    gates = (
        (out_weight_grad,),
        (gu_block_a, ffn_pass),
        (layer_quarter, down_block_b),
        (out_sent, gu_block_b, gu_trade_a[1], down_trade_a[1], down_trade_b[1]),
    )
    core_index, half_rows = t_index % 2, token_count // 2

    def core_rows(value, base, which):
        return lax.dynamic_slice_in_dim(value, base + which * quarter, quarter, 0)

    def chip_rows(part):
        got = swap_core(core_rows(part, 0, 1 - core_index))
        return two_way(core_rows(part, 0, core_index), got).astype(BF)

    grouped = query_low.reshape(token_count, -1, GROUP, HD)
    grad_grouped = mixed_grad.reshape(token_count, -1, GROUP, HD)
    key_grad = jnp.zeros(key_low.shape, F32)
    value_grad = jnp.zeros(value_seq.shape, F32)
    qkv_grad_parts, e_one_parts, query_parts = [], [], []
    for number, ((start, size, first_key, last), log_part, gate) in enumerate(
        zip(reversed(list(spans(token_count))), reversed(log_total), gates)
    ):
        grad_block = tie(grad_grouped[start : start + size], *gate)
        if number == 2:
            grad_block = tie(grad_block, e_one_parts[0])
        if number == 3:
            chip_late = chip_rows(e_one_parts[0])
            grad_block = tie(grad_block, chip_late)
        query_part, key_part, value_part = block_backward(
            grouped[start : start + size],
            key_low[first_key:last],
            value_seq[first_key:last],
            log_part,
            grad_block,
            segment_row,
            start,
            first_key,
        )
        key_grad = key_grad.at[first_key:last].add(key_part)
        value_grad = value_grad.at[first_key:last].add(value_part)
        query_parts.insert(0, query_part)
        if number % 2 == 1:
            span = slice(start, start + half_rows)
            cosine_span, sine_span = cosine_wide[span], -sine_wide[span]
            query_grad = jnp.concatenate(query_parts, axis=0).reshape(half_rows, -1, HD)
            qkv_grad_part = jnp.concatenate(
                [
                    rotate(query_grad, cosine_span, sine_span).reshape(half_rows, -1),
                    rotate(key_grad[span], cosine_span, sine_span).reshape(half_rows, -1),
                    value_grad[span].reshape(half_rows, -1),
                ],
                axis=1,
            ).astype(BF)
            query_parts = []
            qkv_grad_parts.insert(0, qkv_grad_part)
            if number == 1:
                e_one_parts.append(dot_cols(qkv_grad_part, qkv_full, BF))
    qkv_weight_grad = dot_rows(normed, jnp.concatenate(qkv_grad_parts, axis=0), BF)
    e_one_parts.append(dot_cols(tie(qkv_grad_parts[0], qkv_weight_grad), qkv_full, BF))

    chip_early = chip_rows(e_one_parts[1])

    qkv_cut = qkv_weight_grad.reshape(groups, 2, rows, -1)

    def qkv_pick(side):
        def pick(back):
            start = ((z_index - back) % groups, side, 0, 0)
            return lax.dynamic_slice(qkv_cut, start, (1, 1, rows, qkv_cols))[0, 0]

        return pick

    qkv_mine, qkv_other_y = qkv_pick(y_index), qkv_pick(1 - y_index)
    qkv_sent = [swap_y(qkv_other_y(back)) for back in range(1, groups + 1)]

    def qkv_part(back):
        return two_way(qkv_mine(back), qkv_sent[back - 1])

    def tokens_rows(chip_sum, chip_other, start):
        e_one = two_way(chip_sum, chip_other)
        grad_rows = lax.dynamic_slice_in_dim(
            hidden_low, (t_index ^ (start // quarter + core_index)) * quarter, quarter, 0
        ).astype(F32)
        root = core_rows(token_root, start, core_index)
        n_one = core_rows(tokens, start, core_index).astype(F32) * root
        own = grad_rows + root * (e_one - n_one * jnp.mean(e_one * n_one, axis=-1, keepdims=True))
        own = own.astype(BF)
        return own, swap_core(own)

    def core_order(own, other):
        return jnp.where(
            core_index == 0,
            jnp.concatenate([own, other], axis=0),
            jnp.concatenate([other, own], axis=0),
        ).astype(F32)

    late_other, early_other = swap_x(chip_late), swap_x(chip_early)
    layer_x = swap_x(layer_quarter)
    layer_output = absolute(
        [layer_quarter, swap_core(layer_quarter), layer_x, swap_core(tie(layer_x, qkv_weight_grad))],
        BF,
    )
    qkv_send = tie(qkv_part(1).astype(BF), chip_early, out_block, gu_trade_b[1])
    qkv_runs = []
    for step in range(1, groups):
        qkv_runs.append(hop(qkv_send))
        if step == 1:
            late_rows = tokens_rows(chip_late, tie(late_other, qkv_send), half_rows)
        if step < groups - 1:
            qkv_send = (qkv_runs[-1].astype(F32) + qkv_part(step + 1)).astype(BF)
            if step == 1:
                early_rows = tokens_rows(chip_early, tie(early_other, qkv_send), 0)
    qkv_block = ring_end(qkv_runs[-1], qkv_part)
    tokens_grad = jnp.concatenate(
        [core_order(*early_rows), core_order(tie(late_rows[0], qkv_send), late_rows[1])], axis=0
    )

    def all_units(pairs, place):
        pairs = [(mine, tie(got, qkv_send)) for mine, got in pairs]

        def side(which):
            return jnp.concatenate(
                [pair[which][:, place * n : (place + 1) * n] for pair, n in zip(pairs, part_units)],
                axis=1,
            )

        return by_y(side(0), side(1), 1).astype(F32)

    gate_g, up_g = all_units((gu_trade_a, gu_trade_b), 0), all_units((gu_trade_a, gu_trade_b), 1)
    down_weight_grad = all_units((down_trade_a, down_trade_b), 0).T

    attn_gain_part = jnp.sum(
        qkv_block * jnp.concatenate([query_weight, key_weight, value_weight], axis=1).astype(F32),
        axis=1,
    )
    ffn_gain_part = jnp.sum(
        gate_g * gate_weight.astype(F32) + up_g * up_weight.astype(F32), axis=1
    )

    def sum_tensor(value):
        value = value + swap_core(value)
        return value + swap_x(value)

    attn_gain_grad, ffn_gain_grad = sum_tensor(jnp.stack([attn_gain_part, ffn_gain_part]))
    qkv_out = qkv_block * attn_scale
    return (
        layer_output,
        tokens_grad,
        attn_gain_grad,
        qkv_out[:, :q_cols],
        qkv_out[:, q_cols : q_cols + kv_cols],
        qkv_out[:, q_cols + kv_cols :],
        out_grad,
        ffn_gain_grad,
        gate_g * ffn_scale,
        up_g * ffn_scale,
        down_weight_grad,
    )


def solution(mesh):
    return jax.shard_map(
        partial(shards, mesh.shape["dp"], mesh.shape["tensor"]),
        mesh=mesh,
        in_specs=(
            P("dp", None),
            P("dp", None),
            P("dp"),
            P("dp", "tensor"),
            P("dp", "tensor"),
            P("dp", "tensor"),
            P("tensor", "dp"),
            P("dp"),
            P("dp", "tensor"),
            P("dp", "tensor"),
            P("tensor", "dp"),
            P("dp", None),
        ),
        out_specs=(
            P("dp", None),
            P("dp", None),
            P("dp"),
            P("dp", "tensor"),
            P("dp", "tensor"),
            P("dp", "tensor"),
            P("tensor", "dp"),
            P("dp"),
            P("dp", "tensor"),
            P("dp", "tensor"),
            P("tensor", "dp"),
        ),
        check_vma=False,
    )
```

```python
from functools import partial
import math

import jax
import jax.numpy as jnp
from jax import lax
from jax.sharding import PartitionSpec as P

HD = 64
GROUP = 4
epsilon = 1e-05
BF = jnp.bfloat16
F32 = jnp.float32


def rope_tables(segment_row, head_size):
    length = segment_row.shape[0]
    places = jnp.arange(length, dtype=jnp.int32)
    boundary = jnp.concatenate([jnp.ones((1,), dtype=bool), segment_row[1:] != segment_row[:-1]])
    starts = lax.cummax(jnp.where(boundary, places, 0), axis=0)
    position = (places - starts).astype(jnp.float32)
    half_size = head_size // 2
    exponent = jnp.arange(half_size, dtype=jnp.float32) * 2.0 / head_size
    inverse = 1.0 / 500000.0**exponent
    wavelen = 2.0 * math.pi / inverse
    smooth = (8192.0 / wavelen - 1.0) / 3.0
    scaled = jnp.where(
        wavelen < 2048.0,
        inverse,
        jnp.where(
            wavelen > 8192.0, inverse / 32.0, (1.0 - smooth) * inverse / 32.0 + smooth * inverse
        ),
    )
    angles = position[:, None] * scaled[None, :]
    cosine_table = jnp.cos(angles)
    sine_table = jnp.sin(angles)
    return (
        jnp.concatenate([cosine_table, cosine_table], axis=-1),
        jnp.concatenate([sine_table, sine_table], axis=-1),
    )


def rotate(values, cosine_table, sine_table):
    half_size = values.shape[-1] // 2
    turned = jnp.concatenate([-values[..., half_size:], values[..., :half_size]], axis=-1)
    return values * cosine_table + turned * sine_table


def dot_rows(left, right, out=F32):
    return lax.dot_general(
        left, right, (((0,), (0,)), ((), ())), preferred_element_type=F32
    ).astype(out)


def dot_cols(left, right, out=F32):
    return lax.dot_general(
        left, right, (((1,), (1,)), ((), ())), preferred_element_type=F32
    ).astype(out)


def dot(left, right, out=F32):
    return jnp.dot(left, right, preferred_element_type=F32).astype(out)


def tie(value, *others):
    return lax.optimization_barrier((value, *others))[0]


def inverse_root(values):
    return lax.rsqrt(jnp.mean(values * values, axis=-1, keepdims=True) + epsilon)


def spans(length):
    rows = length // 4
    most = length // 2
    for start in range(0, length, rows):
        first = max(0, start - most + 1) // rows * rows
        yield start, rows, first, start + rows


def block_scores(query_block, key_block, segment_row, start, first):
    rows, keys = query_block.shape[0], key_block.shape[0]
    scores = jnp.einsum("qkgd,skd->kgqs", query_block, key_block, preferred_element_type=F32)
    row_ids = start + jnp.arange(rows, dtype=jnp.int32)
    col_ids = first + jnp.arange(keys, dtype=jnp.int32)
    same_doc = segment_row[start : start + rows][:, None] == segment_row[first : first + keys][None, :]
    allowed = same_doc & (col_ids[None, :] <= row_ids[:, None])
    return jnp.where(allowed, scores, -1000000000.0)


def attend_forward(query_seq, key_seq, value_seq, segment_row):
    length, kv_local, head_size = key_seq.shape
    grouped = query_seq.reshape(length, kv_local, -1, head_size)
    mixed_parts = []
    total_parts = []
    for start, rows, first, last in spans(length):
        query_block = grouped[start : start + rows]
        scores = block_scores(query_block, key_seq[first:last], segment_row, start, first)
        row_max = jnp.max(scores, axis=-1, keepdims=True)
        log_total = jnp.log(jnp.sum(jnp.exp(scores - row_max), axis=-1, keepdims=True)) + row_max
        soft_low = jnp.exp(scores - log_total).astype(BF)
        mixed_block = jnp.einsum(
            "kgqs,skd->qkgd", soft_low, value_seq[first:last], preferred_element_type=F32
        )
        mixed_parts.append(mixed_block.reshape(rows, -1).astype(BF))
        total_parts.append(log_total)
    return (jnp.concatenate(mixed_parts, axis=0), total_parts)


def block_backward(query_block, key_block, value_block, log_total, grad_block, segment_row, start, first):
    scores = block_scores(query_block, key_block, segment_row, start, first)
    soft_weights = jnp.exp(scores - log_total)
    soft_grad = jnp.einsum("qkgd,skd->kgqs", grad_block, value_block, preferred_element_type=F32)
    score_grad = (
        soft_weights * (soft_grad - jnp.sum(soft_weights * soft_grad, axis=-1, keepdims=True))
    ).astype(BF)
    query_part = jnp.einsum("kgqs,skd->qkgd", score_grad, key_block, preferred_element_type=F32)
    key_part = jnp.einsum("kgqs,qkgd->skd", score_grad, query_block, preferred_element_type=F32)
    value_part = jnp.einsum(
        "kgqs,qkgd->skd", soft_weights.astype(BF), grad_block, preferred_element_type=F32
    )
    return query_part * query_block.shape[-1] ** (-0.5), key_part, value_part


def shards(
    dp_size,
    tensor_size,
    tokens,
    segment_ids,
    attn_gain,
    query_weight,
    key_weight,
    value_weight,
    output_weight,
    ffn_gain,
    gate_weight,
    up_weight,
    down_weight,
    cotangent,
):
    groups = dp_size // 2
    dp_index = lax.axis_index("dp")
    z_index, y_index = dp_index // 2, dp_index % 2
    t_index = lax.axis_index("tensor")
    token_count, width = tokens.shape
    rows = query_weight.shape[0]
    quarter = token_count // tensor_size
    half_quarter = quarter // 2

    def swap_y(value):
        return lax.ppermute(value, "dp", [(i, i ^ 1) for i in range(dp_size)])

    def swap_x(value):
        return lax.ppermute(value, "tensor", [(i, i ^ 2) for i in range(tensor_size)])

    def swap_core(value):
        return lax.ppermute(value, "tensor", [(i, i ^ 1) for i in range(tensor_size)])

    def hop(value):
        return lax.ppermute(value, "dp", [(i, (i + 2) % dp_size) for i in range(dp_size)])

    def my_half(value, axis, mine):
        size = value.shape[axis] // 2
        which = y_index if mine else 1 - y_index
        return lax.dynamic_slice_in_dim(value, which * size, size, axis)

    def relative(value):
        return jnp.concatenate(
            [
                lax.dynamic_slice_in_dim(value, (t_index ^ j) * quarter, quarter, 0)
                for j in range(tensor_size)
            ],
            axis=0,
        )

    def absolute(pieces, dtype):
        whole = jnp.zeros((quarter * tensor_size, pieces[0].shape[1]), dtype)
        for j, piece in enumerate(pieces):
            whole = lax.dynamic_update_slice(
                whole, piece.astype(dtype), ((t_index ^ j) * quarter, 0)
            )
        return whole

    z_groups = [[i for i in range(dp_size) if i % 2 == side] for side in range(2)]

    def gather_z(value):
        return lax.all_gather(value, "dp", axis_index_groups=z_groups, axis=0, tiled=True)

    def scatter_z(value):
        return lax.psum_scatter(
            value, "dp", axis_index_groups=z_groups, scatter_dimension=0, tiled=True
        )

    def by_y(mine, got, axis):
        return jnp.where(
            y_index == 0,
            jnp.concatenate([mine, got], axis=axis),
            jnp.concatenate([got, mine], axis=axis),
        )

    def pair_rows(mine, got):
        size = mine.shape[0]
        whole = jnp.zeros((2 * size, mine.shape[1]), BF)
        whole = lax.dynamic_update_slice(whole, mine, (y_index * size, 0))
        return lax.dynamic_update_slice(whole, got, ((1 - y_index) * size, 0))

    def interleave(mine, other):
        mine = mine.reshape(groups, 1, rows, -1)
        other = other.reshape(groups, 1, rows, -1)
        return by_y(mine, other, 1).reshape(2 * groups * rows, -1)

    attn_scale = attn_gain.astype(F32)[:, None]
    ffn_scale = ffn_gain.astype(F32)[:, None]

    def scaled(weight, scale):
        return (weight.astype(F32) * scale).astype(BF)

    q_cols, kv_cols = query_weight.shape[1], key_weight.shape[1]
    qkv_cols = q_cols + 2 * kv_cols
    hidden_units = gate_weight.shape[1] // 2
    first_units = hidden_units * 3 // 8
    part_units = (first_units, hidden_units - first_units)
    trio = (scaled(gate_weight, ffn_scale), scaled(up_weight, ffn_scale), down_weight.T)

    def trio_part(side, part):
        start = side * hidden_units + part * first_units
        return jnp.concatenate(
            [lax.dynamic_slice_in_dim(weight, start, part_units[part], 1) for weight in trio], axis=1
        )

    attn_local = jnp.concatenate(
        [
            scaled(jnp.concatenate([query_weight, key_weight, value_weight], axis=1), attn_scale),
            output_weight.T,
        ],
        axis=1,
    )
    attn_z = gather_z(attn_local)
    send_a = tie(trio_part(1 - y_index, 0), attn_local)
    got_a = swap_y(send_a)
    pair_a = pair_rows(trio_part(y_index, 0), got_a)
    full_a = gather_z(tie(pair_a, attn_local))
    got_b = swap_y(tie(trio_part(1 - y_index, 1), got_a))
    pair_b = pair_rows(trio_part(y_index, 1), got_b)
    full_b = gather_z(tie(pair_b, pair_a))
    qkv_z, out_z = attn_z[:, :qkv_cols], attn_z[:, qkv_cols:]
    qkv_other = swap_y(tie(qkv_z, pair_b))
    out_other = swap_y(tie(out_z, qkv_other))
    qkv_full = interleave(qkv_z, qkv_other)
    out_full = interleave(out_z, out_other)

    def quarter_of(value, other):
        return lax.dynamic_slice_in_dim(value, (t_index ^ other) * quarter, quarter, 0)

    cot_own, cot_x = quarter_of(cotangent, 0), quarter_of(cotangent, 2)
    cot_pair = swap_y(tie(jnp.concatenate([cot_own, cot_x], axis=0), out_other))

    tokens_float = tokens.astype(F32)
    token_root = inverse_root(tokens_float)
    normed = (tokens_float * token_root).astype(BF)
    qkv_raw = dot(normed, qkv_full)
    segment_row = segment_ids[0]
    cosine_table, sine_table = rope_tables(segment_row, HD)
    cosine_wide, sine_wide = cosine_table[:, None, :], sine_table[:, None, :]
    query_raw = qkv_raw[:, :q_cols].reshape(token_count, -1, HD)
    key_raw = qkv_raw[:, q_cols : q_cols + kv_cols].reshape(token_count, -1, HD)
    value_seq = qkv_raw[:, q_cols + kv_cols :].astype(BF).reshape(token_count, -1, HD)
    query_low = (rotate(query_raw, cosine_wide, sine_wide) * HD ** (-0.5)).astype(BF)
    key_low = rotate(key_raw, cosine_wide, sine_wide).astype(BF)
    mixed, log_total = attend_forward(query_low, key_low, value_seq, segment_row)
    mixed_rel = relative(mixed)
    attn_part = dot_cols(mixed_rel, out_full, BF)

    def two_way(first, second):
        return first.astype(F32) + second.astype(F32)

    def scatter_tensor(part):
        send = jnp.concatenate([part[quarter : 2 * quarter], part[3 * quarter :]], axis=0)
        got = swap_core(send)
        keep = two_way(part[:quarter], got[:quarter])
        pass_on = two_way(part[2 * quarter : 3 * quarter], got[quarter:]).astype(BF)
        return keep + swap_x(pass_on).astype(F32)

    def gather_tensor(piece):
        from_core = swap_core(piece)
        from_x = swap_x(piece)
        from_both = swap_core(from_x)
        return [piece, from_core, from_x, from_both]

    def my_quarter(value):
        return lax.dynamic_slice_in_dim(value, t_index * quarter, quarter, 0)

    tokens_quarter = my_quarter(tokens).astype(F32)
    hidden = tokens_quarter + scatter_tensor(attn_part)
    hidden_root = inverse_root(hidden)
    n_two = (hidden * hidden_root).astype(BF)

    first, second = n_two[:half_quarter], n_two[half_quarter:]
    top = jnp.concatenate([first, swap_x(first)], axis=0)
    low = jnp.concatenate([second, swap_y(second)], axis=0)
    top, low = lax.optimization_barrier((top, low))
    n_held = jnp.concatenate([top, swap_y(top), low, swap_x(low)], axis=0)
    n_held = tie(n_held, full_a)
    n_all = jnp.concatenate([n_held, swap_core(n_held)], axis=0)

    cot_pair = tie(cot_pair, n_two)
    cot_y, cot_yx = cot_pair[:quarter], cot_pair[quarter:]
    cot_held = jnp.concatenate(
        [v[:half_quarter] for v in (cot_own, cot_x, cot_y, cot_yx)]
        + [v[half_quarter:] for v in (cot_own, cot_y, cot_x, cot_yx)],
        axis=0,
    )
    cot_all = jnp.concatenate([cot_held, swap_core(cot_held)], axis=0)


    side_rows = 4 * quarter

    def pair_sends(part, got):
        def kept(start):
            return two_way(part[start : start + quarter], got[start : start + quarter])

        keeps = (kept(0), kept(2 * quarter))
        return keeps, (kept(quarter).astype(BF), kept(3 * quarter).astype(BF))

    def pair_pass(keeps, sends):
        top_sum = keeps[0] + swap_y(sends[0]).astype(F32)
        low_sum = keeps[1] + swap_x(sends[1]).astype(F32)
        passes = (top_sum[half_quarter:].astype(BF), low_sum[half_quarter:].astype(BF))
        return (top_sum[:half_quarter], low_sum[:half_quarter]), passes

    def pair_sum(keeps, passes):
        return jnp.concatenate(
            [keeps[0] + swap_x(passes[0]).astype(F32), keeps[1] + swap_y(passes[1]).astype(F32)],
            axis=0,
        )

    def units(full, rows_all):
        count = full.shape[1] // 3
        gu = dot(rows_all, full[:, : 2 * count], BF)
        gate_values = gu[:, :count].astype(F32)
        up_values = gu[:, count:].astype(F32)
        sig = jax.nn.sigmoid(gate_values)
        silu = gate_values * sig
        return gate_values, up_values, sig, silu, (silu * up_values).astype(BF)

    def units_grad(full, parts, cot_rows):
        gate_values, up_values, sig, silu, _ = parts
        active_grad = dot(cot_rows, full[:, full.shape[1] // 3 * 2 :])
        gate_grad = active_grad * up_values * (sig * (1.0 + gate_values * (1.0 - sig)))
        return jnp.concatenate([gate_grad.astype(BF), (active_grad * silu).astype(BF)], axis=1)

    parts_a = units(full_a, n_all)
    active_a = parts_a[-1]
    down_grad_a = dot_rows(cot_all, active_a, BF)
    down_block_a = scatter_z(down_grad_a)
    gu_grad_a = units_grad(full_a, parts_a, tie(cot_all, down_grad_a))
    gu_weight_grad_a = dot_rows(n_all, gu_grad_a, BF)
    gu_block_a = scatter_z(gu_weight_grad_a)
    gu_a, gu_b = (v[:, : 2 * n] for v, n in zip((full_a, full_b), part_units))
    down_a, down_b = (v[:, 2 * n :] for v, n in zip((full_a, full_b), part_units))
    e_part_a = dot_cols(tie(gu_grad_a, gu_weight_grad_a), gu_a, BF)
    ffn_part_a = dot_cols(tie(active_a, e_part_a), down_a, BF)

    parts_b = units(full_b, tie(n_all, ffn_part_a))
    active_b = parts_b[-1]
    gu_grad_b = units_grad(full_b, parts_b, cot_all)
    own, other = slice(0, side_rows), slice(side_rows, 2 * side_rows)
    e_cross = (dot_cols(gu_grad_b[other], gu_b) + e_part_a[other].astype(F32)).astype(BF)
    e_got = swap_core(e_cross)
    e_part = dot_cols(tie(gu_grad_b, e_cross)[own], gu_b) + e_part_a[own].astype(F32)
    e_part = e_part.astype(BF)
    down_grad_b = dot_rows(cot_all, tie(active_b, e_part, down_block_a), BF)
    down_block_b = scatter_z(down_grad_b)
    e_keeps, e_sends = pair_sends(tie(e_part, e_cross), e_got)
    gu_weight_grad_b = dot_rows(n_all, tie(gu_grad_b, down_grad_b, *e_sends), BF)
    gu_block_b = scatter_z(gu_weight_grad_b)
    ffn_cross = dot_cols(tie(active_b, gu_weight_grad_b)[other], down_b)
    ffn_cross = (ffn_cross + ffn_part_a[other].astype(F32)).astype(BF)
    ffn_got = swap_core(ffn_cross)
    e_keeps, e_passes = pair_pass(tuple(tie(v, ffn_cross) for v in e_keeps), e_sends)
    ffn_part = dot_cols(tie(active_b, *e_passes)[own], down_b)
    ffn_part = (ffn_part + ffn_part_a[own].astype(F32)).astype(BF)
    e_two = pair_sum(tuple(tie(v, ffn_part) for v in e_keeps), e_passes)
    n_hidden = hidden * hidden_root
    cot_quarter = my_quarter(cotangent).astype(F32)
    hidden_grad = cot_quarter + hidden_root * (
        e_two - n_hidden * jnp.mean(e_two * n_hidden, axis=-1, keepdims=True)
    )
    hidden_low = jnp.concatenate(gather_tensor(hidden_grad.astype(BF)), axis=0)

    def pair_rows_of(part, got, blocks):
        return jnp.concatenate(
            [
                two_way(
                    part[i * half_quarter : (i + 1) * half_quarter],
                    got[i * half_quarter : (i + 1) * half_quarter],
                )
                for i in blocks
            ],
            axis=0,
        )

    ffn_send = pair_rows_of(ffn_part, ffn_got, (2, 5, 3, 7)).astype(BF)
    ffn_keep = pair_rows_of(ffn_part, ffn_got, (0, 4, 1, 6))
    hidden_low = tie(hidden_low, ffn_send)
    ffn_sum = ffn_keep + swap_y(ffn_send).astype(F32)
    ffn_pass = ffn_sum[quarter:].astype(BF)
    layer_quarter = (hidden + ffn_sum[:quarter] + swap_x(ffn_pass).astype(F32)).astype(BF)

    def ring_end(received, block):
        return received.astype(F32) + block(groups)

    mixed_grad_rel = dot(hidden_low, out_full, BF)
    out_weight_grad = dot_rows(hidden_low, tie(mixed_rel, mixed_grad_rel), BF)
    cut = out_weight_grad.reshape(groups, 2, rows, -1)
    out_mine = lax.dynamic_index_in_dim(cut, y_index, 1, keepdims=False)
    out_send = lax.dynamic_index_in_dim(cut, 1 - y_index, 1, keepdims=False)
    out_sent = swap_y(tie(out_send, ffn_pass))
    out_both = two_way(out_mine, out_sent).astype(BF).reshape(groups * rows, -1)
    out_block = scatter_z(tie(out_both, gu_block_b))
    out_grad = out_block.astype(F32).T
    mixed_grad = absolute(
        [mixed_grad_rel[j * quarter : (j + 1) * quarter] for j in range(tensor_size)], BF
    )
    def trade(block):
        return my_half(block, 0, True), swap_y(my_half(block, 0, False))

    gu_trade_a, down_trade_a = trade(gu_block_a), trade(down_block_a)
    down_trade_b, gu_trade_b = trade(tie(down_block_b, mixed_grad_rel)), trade(gu_block_b)
    gates = (
        (out_weight_grad,),
        (gu_block_a,),
        (ffn_pass, down_block_b),
        (layer_quarter, out_sent, gu_block_b, gu_trade_a[1], down_trade_a[1], down_trade_b[1]),
    )
    core_index, half_rows = t_index % 2, token_count // 2

    def core_rows(value, base, which):
        return lax.dynamic_slice_in_dim(value, base + which * quarter, quarter, 0)

    def chip_rows(part):
        got = swap_core(core_rows(part, 0, 1 - core_index))
        return two_way(core_rows(part, 0, core_index), got).astype(BF)

    grouped = query_low.reshape(token_count, -1, GROUP, HD)
    grad_grouped = mixed_grad.reshape(token_count, -1, GROUP, HD)
    key_grad = jnp.zeros(key_low.shape, F32)
    value_grad = jnp.zeros(value_seq.shape, F32)
    qkv_grad_parts, e_one_parts, query_parts = [], [], []
    for number, ((start, size, first_key, last), log_part, gate) in enumerate(
        zip(reversed(list(spans(token_count))), reversed(log_total), gates)
    ):
        grad_block = tie(grad_grouped[start : start + size], *gate)
        if number == 2:
            grad_block = tie(grad_block, e_one_parts[0])
        if number == 3:
            chip_late = chip_rows(e_one_parts[0])
            grad_block = tie(grad_block, chip_late)
        query_part, key_part, value_part = block_backward(
            grouped[start : start + size],
            key_low[first_key:last],
            value_seq[first_key:last],
            log_part,
            grad_block,
            segment_row,
            start,
            first_key,
        )
        key_grad = key_grad.at[first_key:last].add(key_part)
        value_grad = value_grad.at[first_key:last].add(value_part)
        query_parts.insert(0, query_part)
        if number % 2 == 1:
            span = slice(start, start + half_rows)
            cosine_span, sine_span = cosine_wide[span], -sine_wide[span]
            query_grad = jnp.concatenate(query_parts, axis=0).reshape(half_rows, -1, HD)
            qkv_grad_part = jnp.concatenate(
                [
                    rotate(query_grad, cosine_span, sine_span).reshape(half_rows, -1),
                    rotate(key_grad[span], cosine_span, sine_span).reshape(half_rows, -1),
                    value_grad[span].reshape(half_rows, -1),
                ],
                axis=1,
            ).astype(BF)
            query_parts = []
            qkv_grad_parts.insert(0, qkv_grad_part)
            if number == 1:
                e_one_parts.append(dot_cols(qkv_grad_part, qkv_full, BF))
    qkv_weight_grad = dot_rows(normed, jnp.concatenate(qkv_grad_parts, axis=0), BF)
    e_one_parts.append(dot_cols(tie(qkv_grad_parts[0], qkv_weight_grad), qkv_full, BF))

    chip_early = chip_rows(e_one_parts[1])

    qkv_cut = qkv_weight_grad.reshape(groups, 2, rows, -1)

    def qkv_pick(side):
        def pick(back):
            start = ((z_index - back) % groups, side, 0, 0)
            return lax.dynamic_slice(qkv_cut, start, (1, 1, rows, qkv_cols))[0, 0]

        return pick

    qkv_mine, qkv_other_y = qkv_pick(y_index), qkv_pick(1 - y_index)
    qkv_sent = [swap_y(qkv_other_y(back)) for back in range(1, groups + 1)]

    def qkv_part(back):
        return two_way(qkv_mine(back), qkv_sent[back - 1])

    def tokens_rows(chip_sum, chip_other, start):
        e_one = two_way(chip_sum, chip_other)
        grad_rows = lax.dynamic_slice_in_dim(
            hidden_low, (t_index ^ (start // quarter + core_index)) * quarter, quarter, 0
        ).astype(F32)
        root = core_rows(token_root, start, core_index)
        n_one = core_rows(tokens, start, core_index).astype(F32) * root
        own = grad_rows + root * (e_one - n_one * jnp.mean(e_one * n_one, axis=-1, keepdims=True))
        own = own.astype(BF)
        return own, swap_core(own)

    def core_order(own, other):
        return jnp.where(
            core_index == 0,
            jnp.concatenate([own, other], axis=0),
            jnp.concatenate([other, own], axis=0),
        ).astype(F32)

    late_other, early_other = swap_x(chip_late), swap_x(chip_early)
    layer_x = swap_x(layer_quarter)
    layer_output = absolute(
        [layer_quarter, swap_core(layer_quarter), layer_x, swap_core(tie(layer_x, qkv_weight_grad))],
        BF,
    )
    qkv_send = tie(qkv_part(1).astype(BF), chip_early, out_block)
    qkv_runs = []
    for step in range(1, groups):
        qkv_runs.append(hop(qkv_send))
        if step == 1:
            late_rows = tokens_rows(chip_late, tie(late_other, qkv_send), half_rows)
        if step < groups - 1:
            qkv_send = (qkv_runs[-1].astype(F32) + qkv_part(step + 1)).astype(BF)
            if step == 1:
                qkv_send = tie(qkv_send, gu_trade_b[1])
                early_rows = tokens_rows(chip_early, tie(early_other, qkv_send), 0)
    tokens_grad = jnp.concatenate(
        [core_order(*early_rows), core_order(tie(late_rows[0], qkv_send), late_rows[1])], axis=0
    )
    qkv_block = ring_end(tie(qkv_runs[-1], tokens_grad), qkv_part)

    def all_units(pairs, place):
        pairs = [(mine, tie(got, qkv_send)) for mine, got in pairs]

        def side(which):
            return jnp.concatenate(
                [pair[which][:, place * n : (place + 1) * n] for pair, n in zip(pairs, part_units)],
                axis=1,
            )

        return by_y(side(0), side(1), 1).astype(F32)

    gate_g, up_g = all_units((gu_trade_a, gu_trade_b), 0), all_units((gu_trade_a, gu_trade_b), 1)
    down_weight_grad = all_units((down_trade_a, down_trade_b), 0).T

    attn_gain_part = jnp.sum(
        qkv_block * jnp.concatenate([query_weight, key_weight, value_weight], axis=1).astype(F32),
        axis=1,
    )
    ffn_gain_part = jnp.sum(
        gate_g * gate_weight.astype(F32) + up_g * up_weight.astype(F32), axis=1
    )

    def sum_tensor(value):
        value = value + swap_core(value)
        return value + swap_x(value)

    attn_gain_grad, ffn_gain_grad = sum_tensor(jnp.stack([attn_gain_part, ffn_gain_part]))
    qkv_out = qkv_block * attn_scale
    return (
        layer_output,
        tokens_grad,
        attn_gain_grad,
        qkv_out[:, :q_cols],
        qkv_out[:, q_cols : q_cols + kv_cols],
        qkv_out[:, q_cols + kv_cols :],
        out_grad,
        ffn_gain_grad,
        gate_g * ffn_scale,
        up_g * ffn_scale,
        down_weight_grad,
    )


def solution(mesh):
    return jax.shard_map(
        partial(shards, mesh.shape["dp"], mesh.shape["tensor"]),
        mesh=mesh,
        in_specs=(
            P("dp", None),
            P("dp", None),
            P("dp"),
            P("dp", "tensor"),
            P("dp", "tensor"),
            P("dp", "tensor"),
            P("tensor", "dp"),
            P("dp"),
            P("dp", "tensor"),
            P("dp", "tensor"),
            P("tensor", "dp"),
            P("dp", None),
        ),
        out_specs=(
            P("dp", None),
            P("dp", None),
            P("dp"),
            P("dp", "tensor"),
            P("dp", "tensor"),
            P("dp", "tensor"),
            P("tensor", "dp"),
            P("dp"),
            P("dp", "tensor"),
            P("dp", "tensor"),
            P("tensor", "dp"),
        ),
        check_vma=False,
    )
```

```python
from functools import partial
import math

import jax
import jax.numpy as jnp
from jax import lax
from jax.sharding import PartitionSpec as P

HD = 64
GROUP = 4
epsilon = 1e-05
BF = jnp.bfloat16
F32 = jnp.float32


def rope_tables(segment_row, head_size):
    length = segment_row.shape[0]
    places = jnp.arange(length, dtype=jnp.int32)
    boundary = jnp.concatenate([jnp.ones((1,), dtype=bool), segment_row[1:] != segment_row[:-1]])
    starts = lax.cummax(jnp.where(boundary, places, 0), axis=0)
    position = (places - starts).astype(jnp.float32)
    half_size = head_size // 2
    exponent = jnp.arange(half_size, dtype=jnp.float32) * 2.0 / head_size
    inverse = 1.0 / 500000.0**exponent
    wavelen = 2.0 * math.pi / inverse
    smooth = (8192.0 / wavelen - 1.0) / 3.0
    scaled = jnp.where(
        wavelen < 2048.0,
        inverse,
        jnp.where(
            wavelen > 8192.0, inverse / 32.0, (1.0 - smooth) * inverse / 32.0 + smooth * inverse
        ),
    )
    angles = position[:, None] * scaled[None, :]
    cosine_table = jnp.cos(angles)
    sine_table = jnp.sin(angles)
    return (
        jnp.concatenate([cosine_table, cosine_table], axis=-1),
        jnp.concatenate([sine_table, sine_table], axis=-1),
    )


def rotate(values, cosine_table, sine_table):
    half_size = values.shape[-1] // 2
    turned = jnp.concatenate([-values[..., half_size:], values[..., :half_size]], axis=-1)
    return values * cosine_table + turned * sine_table


def dot_rows(left, right, out=F32):
    return lax.dot_general(
        left, right, (((0,), (0,)), ((), ())), preferred_element_type=F32
    ).astype(out)


def dot_cols(left, right, out=F32):
    return lax.dot_general(
        left, right, (((1,), (1,)), ((), ())), preferred_element_type=F32
    ).astype(out)


def dot(left, right, out=F32):
    return jnp.dot(left, right, preferred_element_type=F32).astype(out)


def tie(value, *others):
    return lax.optimization_barrier((value, *others))[0]


def inverse_root(values):
    return lax.rsqrt(jnp.mean(values * values, axis=-1, keepdims=True) + epsilon)


def spans(length):
    rows = length // 4
    most = length // 2
    for start in range(0, length, rows):
        first = max(0, start - most + 1) // rows * rows
        yield start, rows, first, start + rows


def block_scores(query_block, key_block, segment_row, start, first):
    rows, keys = query_block.shape[0], key_block.shape[0]
    scores = jnp.einsum("qkgd,skd->kgqs", query_block, key_block, preferred_element_type=F32)
    row_ids = start + jnp.arange(rows, dtype=jnp.int32)
    col_ids = first + jnp.arange(keys, dtype=jnp.int32)
    same_doc = segment_row[start : start + rows][:, None] == segment_row[first : first + keys][None, :]
    allowed = same_doc & (col_ids[None, :] <= row_ids[:, None])
    return jnp.where(allowed, scores, -1000000000.0)


def attend_forward(query_seq, key_seq, value_seq, segment_row):
    length, kv_local, head_size = key_seq.shape
    grouped = query_seq.reshape(length, kv_local, -1, head_size)
    mixed_parts = []
    total_parts = []
    for start, rows, first, last in spans(length):
        query_block = grouped[start : start + rows]
        scores = block_scores(query_block, key_seq[first:last], segment_row, start, first)
        row_max = jnp.max(scores, axis=-1, keepdims=True)
        log_total = jnp.log(jnp.sum(jnp.exp(scores - row_max), axis=-1, keepdims=True)) + row_max
        soft_low = jnp.exp(scores - log_total).astype(BF)
        mixed_block = jnp.einsum(
            "kgqs,skd->qkgd", soft_low, value_seq[first:last], preferred_element_type=F32
        )
        mixed_parts.append(mixed_block.reshape(rows, -1).astype(BF))
        total_parts.append(log_total)
    return (jnp.concatenate(mixed_parts, axis=0), total_parts)


def block_backward(query_block, key_block, value_block, log_total, grad_block, segment_row, start, first):
    scores = block_scores(query_block, key_block, segment_row, start, first)
    soft_weights = jnp.exp(scores - log_total)
    soft_grad = jnp.einsum("qkgd,skd->kgqs", grad_block, value_block, preferred_element_type=F32)
    score_grad = (
        soft_weights * (soft_grad - jnp.sum(soft_weights * soft_grad, axis=-1, keepdims=True))
    ).astype(BF)
    query_part = jnp.einsum("kgqs,skd->qkgd", score_grad, key_block, preferred_element_type=F32)
    key_part = jnp.einsum("kgqs,qkgd->skd", score_grad, query_block, preferred_element_type=F32)
    value_part = jnp.einsum(
        "kgqs,qkgd->skd", soft_weights.astype(BF), grad_block, preferred_element_type=F32
    )
    return query_part * query_block.shape[-1] ** (-0.5), key_part, value_part


def shards(
    dp_size,
    tensor_size,
    tokens,
    segment_ids,
    attn_gain,
    query_weight,
    key_weight,
    value_weight,
    output_weight,
    ffn_gain,
    gate_weight,
    up_weight,
    down_weight,
    cotangent,
):
    groups = dp_size // 2
    dp_index = lax.axis_index("dp")
    z_index, y_index = dp_index // 2, dp_index % 2
    t_index = lax.axis_index("tensor")
    token_count, width = tokens.shape
    rows = query_weight.shape[0]
    quarter = token_count // tensor_size
    half_quarter = quarter // 2

    def swap_y(value):
        return lax.ppermute(value, "dp", [(i, i ^ 1) for i in range(dp_size)])

    def swap_x(value):
        return lax.ppermute(value, "tensor", [(i, i ^ 2) for i in range(tensor_size)])

    def swap_core(value):
        return lax.ppermute(value, "tensor", [(i, i ^ 1) for i in range(tensor_size)])

    def hop(value):
        return lax.ppermute(value, "dp", [(i, (i + 2) % dp_size) for i in range(dp_size)])

    def my_half(value, axis, mine):
        size = value.shape[axis] // 2
        which = y_index if mine else 1 - y_index
        return lax.dynamic_slice_in_dim(value, which * size, size, axis)

    def relative(value):
        return jnp.concatenate(
            [
                lax.dynamic_slice_in_dim(value, (t_index ^ j) * quarter, quarter, 0)
                for j in range(tensor_size)
            ],
            axis=0,
        )

    def absolute(pieces, dtype):
        whole = jnp.zeros((quarter * tensor_size, pieces[0].shape[1]), dtype)
        for j, piece in enumerate(pieces):
            whole = lax.dynamic_update_slice(
                whole, piece.astype(dtype), ((t_index ^ j) * quarter, 0)
            )
        return whole

    z_groups = [[i for i in range(dp_size) if i % 2 == side] for side in range(2)]

    def gather_z(value):
        return lax.all_gather(value, "dp", axis_index_groups=z_groups, axis=0, tiled=True)

    def scatter_z(value):
        return lax.psum_scatter(
            value, "dp", axis_index_groups=z_groups, scatter_dimension=0, tiled=True
        )

    def by_y(mine, got, axis):
        return jnp.where(
            y_index == 0,
            jnp.concatenate([mine, got], axis=axis),
            jnp.concatenate([got, mine], axis=axis),
        )

    def pair_rows(mine, got):
        size = mine.shape[0]
        whole = jnp.zeros((2 * size, mine.shape[1]), BF)
        whole = lax.dynamic_update_slice(whole, mine, (y_index * size, 0))
        return lax.dynamic_update_slice(whole, got, ((1 - y_index) * size, 0))

    def interleave(mine, other):
        mine = mine.reshape(groups, 1, rows, -1)
        other = other.reshape(groups, 1, rows, -1)
        return by_y(mine, other, 1).reshape(2 * groups * rows, -1)

    attn_scale = attn_gain.astype(F32)[:, None]
    ffn_scale = ffn_gain.astype(F32)[:, None]

    def scaled(weight, scale):
        return (weight.astype(F32) * scale).astype(BF)

    q_cols, kv_cols = query_weight.shape[1], key_weight.shape[1]
    qkv_cols = q_cols + 2 * kv_cols
    hidden_units = gate_weight.shape[1] // 2
    first_units = hidden_units * 3 // 8
    part_units = (first_units, hidden_units - first_units)
    trio = (scaled(gate_weight, ffn_scale), scaled(up_weight, ffn_scale), down_weight.T)

    def trio_part(side, part):
        start = side * hidden_units + part * first_units
        return jnp.concatenate(
            [lax.dynamic_slice_in_dim(weight, start, part_units[part], 1) for weight in trio], axis=1
        )

    attn_local = jnp.concatenate(
        [
            scaled(jnp.concatenate([query_weight, key_weight, value_weight], axis=1), attn_scale),
            output_weight.T,
        ],
        axis=1,
    )
    attn_z = gather_z(attn_local)
    send_a = tie(trio_part(1 - y_index, 0), attn_local)
    got_a = swap_y(send_a)
    pair_a = pair_rows(trio_part(y_index, 0), got_a)
    full_a = gather_z(tie(pair_a, attn_local))
    got_b = swap_y(tie(trio_part(1 - y_index, 1), got_a))
    pair_b = pair_rows(trio_part(y_index, 1), got_b)
    full_b = gather_z(tie(pair_b, pair_a))
    qkv_z, out_z = attn_z[:, :qkv_cols], attn_z[:, qkv_cols:]
    qkv_other = swap_y(tie(qkv_z, pair_b))
    out_other = swap_y(tie(out_z, qkv_other))
    qkv_full = interleave(qkv_z, qkv_other)
    out_full = interleave(out_z, out_other)

    def quarter_of(value, other):
        return lax.dynamic_slice_in_dim(value, (t_index ^ other) * quarter, quarter, 0)

    cot_own, cot_x = quarter_of(cotangent, 0), quarter_of(cotangent, 2)
    cot_pair = swap_y(tie(jnp.concatenate([cot_own, cot_x], axis=0), out_other))

    tokens_float = tokens.astype(F32)
    token_root = inverse_root(tokens_float)
    normed = (tokens_float * token_root).astype(BF)
    qkv_raw = dot(normed, qkv_full)
    segment_row = segment_ids[0]
    cosine_table, sine_table = rope_tables(segment_row, HD)
    cosine_wide, sine_wide = cosine_table[:, None, :], sine_table[:, None, :]
    query_raw = qkv_raw[:, :q_cols].reshape(token_count, -1, HD)
    key_raw = qkv_raw[:, q_cols : q_cols + kv_cols].reshape(token_count, -1, HD)
    value_seq = qkv_raw[:, q_cols + kv_cols :].astype(BF).reshape(token_count, -1, HD)
    query_low = (rotate(query_raw, cosine_wide, sine_wide) * HD ** (-0.5)).astype(BF)
    key_low = rotate(key_raw, cosine_wide, sine_wide).astype(BF)
    mixed, log_total = attend_forward(query_low, key_low, value_seq, segment_row)
    mixed_rel = relative(mixed)
    attn_part = dot_cols(mixed_rel, out_full, BF)

    def two_way(first, second):
        return first.astype(F32) + second.astype(F32)

    def scatter_tensor(part):
        send = jnp.concatenate([part[quarter : 2 * quarter], part[3 * quarter :]], axis=0)
        got = swap_core(send)
        keep = two_way(part[:quarter], got[:quarter])
        pass_on = two_way(part[2 * quarter : 3 * quarter], got[quarter:]).astype(BF)
        return keep + swap_x(pass_on).astype(F32)

    def gather_tensor(piece):
        from_core = swap_core(piece)
        from_x = swap_x(piece)
        from_both = swap_core(from_x)
        return [piece, from_core, from_x, from_both]

    def my_quarter(value):
        return lax.dynamic_slice_in_dim(value, t_index * quarter, quarter, 0)

    tokens_quarter = my_quarter(tokens).astype(F32)
    hidden = tokens_quarter + scatter_tensor(attn_part)
    hidden_root = inverse_root(hidden)
    n_two = (hidden * hidden_root).astype(BF)

    first, second = n_two[:half_quarter], n_two[half_quarter:]
    top = jnp.concatenate([first, swap_x(first)], axis=0)
    low = jnp.concatenate([second, swap_y(second)], axis=0)
    top, low = lax.optimization_barrier((top, low))
    n_held = jnp.concatenate([top, swap_y(top), low, swap_x(low)], axis=0)
    n_held = tie(n_held, full_a)
    n_all = jnp.concatenate([n_held, swap_core(n_held)], axis=0)

    cot_pair = tie(cot_pair, top, low)
    cot_y, cot_yx = cot_pair[:quarter], cot_pair[quarter:]
    cot_held = jnp.concatenate(
        [v[:half_quarter] for v in (cot_own, cot_x, cot_y, cot_yx)]
        + [v[half_quarter:] for v in (cot_own, cot_y, cot_x, cot_yx)],
        axis=0,
    )
    cot_all = jnp.concatenate([cot_held, swap_core(cot_held)], axis=0)


    side_rows = 4 * quarter

    def pair_sends(part, got):
        def kept(start):
            return two_way(part[start : start + quarter], got[start : start + quarter])

        keeps = (kept(0), kept(2 * quarter))
        return keeps, (kept(quarter).astype(BF), kept(3 * quarter).astype(BF))

    def pair_pass(keeps, sends):
        top_sum = keeps[0] + swap_y(sends[0]).astype(F32)
        low_sum = keeps[1] + swap_x(sends[1]).astype(F32)
        passes = (top_sum[half_quarter:].astype(BF), low_sum[half_quarter:].astype(BF))
        return (top_sum[:half_quarter], low_sum[:half_quarter]), passes

    def pair_sum(keeps, passes):
        return jnp.concatenate(
            [keeps[0] + swap_x(passes[0]).astype(F32), keeps[1] + swap_y(passes[1]).astype(F32)],
            axis=0,
        )

    def units(full, rows_all):
        count = full.shape[1] // 3
        gu = dot(rows_all, full[:, : 2 * count], BF)
        gate_values = gu[:, :count].astype(F32)
        up_values = gu[:, count:].astype(F32)
        sig = jax.nn.sigmoid(gate_values)
        silu = gate_values * sig
        return gate_values, up_values, sig, silu, (silu * up_values).astype(BF)

    def units_grad(full, parts, cot_rows):
        gate_values, up_values, sig, silu, _ = parts
        active_grad = dot(cot_rows, full[:, full.shape[1] // 3 * 2 :])
        gate_grad = active_grad * up_values * (sig * (1.0 + gate_values * (1.0 - sig)))
        return jnp.concatenate([gate_grad.astype(BF), (active_grad * silu).astype(BF)], axis=1)

    parts_a = units(full_a, n_all)
    active_a = parts_a[-1]
    down_grad_a = dot_rows(cot_all, active_a, BF)
    down_block_a = scatter_z(down_grad_a)
    gu_grad_a = units_grad(full_a, parts_a, tie(cot_all, down_grad_a))
    gu_weight_grad_a = dot_rows(n_all, gu_grad_a, BF)
    gu_block_a = scatter_z(gu_weight_grad_a)
    gu_a, gu_b = (v[:, : 2 * n] for v, n in zip((full_a, full_b), part_units))
    down_a, down_b = (v[:, 2 * n :] for v, n in zip((full_a, full_b), part_units))
    e_part_a = dot_cols(tie(gu_grad_a, gu_weight_grad_a), gu_a, BF)
    ffn_part_a = dot_cols(tie(active_a, e_part_a), down_a, BF)

    parts_b = units(full_b, tie(n_all, ffn_part_a))
    active_b = parts_b[-1]
    gu_grad_b = units_grad(full_b, parts_b, cot_all)
    own, other = slice(0, side_rows), slice(side_rows, 2 * side_rows)
    e_cross = (dot_cols(gu_grad_b[other], gu_b) + e_part_a[other].astype(F32)).astype(BF)
    e_got = swap_core(e_cross)
    e_part = dot_cols(tie(gu_grad_b, e_cross)[own], gu_b) + e_part_a[own].astype(F32)
    e_part = e_part.astype(BF)
    down_grad_b = dot_rows(cot_all, tie(active_b, e_part, down_block_a), BF)
    down_block_b = scatter_z(down_grad_b)
    e_keeps, e_sends = pair_sends(tie(e_part, e_cross), e_got)
    gu_weight_grad_b = dot_rows(n_all, tie(gu_grad_b, down_grad_b, *e_sends), BF)
    gu_block_b = scatter_z(gu_weight_grad_b)
    ffn_cross = dot_cols(tie(active_b, gu_weight_grad_b)[other], down_b)
    ffn_cross = (ffn_cross + ffn_part_a[other].astype(F32)).astype(BF)
    ffn_got = swap_core(ffn_cross)
    e_keeps, e_passes = pair_pass(tuple(tie(v, ffn_cross) for v in e_keeps), e_sends)
    ffn_part = dot_cols(tie(active_b, *e_passes)[own], down_b)
    ffn_part = (ffn_part + ffn_part_a[own].astype(F32)).astype(BF)
    e_two = pair_sum(tuple(tie(v, ffn_part) for v in e_keeps), e_passes)
    n_hidden = hidden * hidden_root
    cot_quarter = my_quarter(cotangent).astype(F32)
    hidden_grad = cot_quarter + hidden_root * (
        e_two - n_hidden * jnp.mean(e_two * n_hidden, axis=-1, keepdims=True)
    )
    hidden_low = jnp.concatenate(gather_tensor(hidden_grad.astype(BF)), axis=0)

    def pair_rows_of(part, got, blocks):
        return jnp.concatenate(
            [
                two_way(
                    part[i * half_quarter : (i + 1) * half_quarter],
                    got[i * half_quarter : (i + 1) * half_quarter],
                )
                for i in blocks
            ],
            axis=0,
        )

    ffn_send = pair_rows_of(ffn_part, ffn_got, (2, 5, 3, 7)).astype(BF)
    ffn_keep = pair_rows_of(ffn_part, ffn_got, (0, 4, 1, 6))
    hidden_low = tie(hidden_low, ffn_send)
    ffn_sum = ffn_keep + swap_y(ffn_send).astype(F32)
    ffn_pass = ffn_sum[quarter:].astype(BF)
    layer_quarter = (hidden + ffn_sum[:quarter] + swap_x(ffn_pass).astype(F32)).astype(BF)

    def ring_end(received, block):
        return received.astype(F32) + block(groups)

    mixed_grad_rel = dot(hidden_low, out_full, BF)
    out_weight_grad = dot_rows(hidden_low, tie(mixed_rel, mixed_grad_rel), BF)
    cut = out_weight_grad.reshape(groups, 2, rows, -1)
    out_mine = lax.dynamic_index_in_dim(cut, y_index, 1, keepdims=False)
    out_send = lax.dynamic_index_in_dim(cut, 1 - y_index, 1, keepdims=False)
    out_sent = swap_y(tie(out_send, ffn_pass))
    out_both = two_way(out_mine, out_sent).astype(BF).reshape(groups * rows, -1)
    out_block = scatter_z(tie(out_both, gu_block_b))
    out_grad = out_block.astype(F32).T
    mixed_grad = absolute(
        [mixed_grad_rel[j * quarter : (j + 1) * quarter] for j in range(tensor_size)], BF
    )
    def trade(block):
        return my_half(block, 0, True), swap_y(my_half(block, 0, False))

    gu_trade_a, down_trade_a = trade(gu_block_a), trade(down_block_a)
    down_trade_b, gu_trade_b = trade(tie(down_block_b, mixed_grad_rel)), trade(gu_block_b)
    gates = (
        (out_weight_grad,),
        (gu_block_a,),
        (ffn_pass, down_block_b),
        (layer_quarter, out_sent, gu_block_b, gu_trade_a[1], down_trade_a[1], down_trade_b[1]),
    )
    core_index, half_rows = t_index % 2, token_count // 2

    def core_rows(value, base, which):
        return lax.dynamic_slice_in_dim(value, base + which * quarter, quarter, 0)

    def chip_rows(part):
        got = swap_core(core_rows(part, 0, 1 - core_index))
        return two_way(core_rows(part, 0, core_index), got).astype(BF)

    grouped = query_low.reshape(token_count, -1, GROUP, HD)
    grad_grouped = mixed_grad.reshape(token_count, -1, GROUP, HD)
    key_grad = jnp.zeros(key_low.shape, F32)
    value_grad = jnp.zeros(value_seq.shape, F32)
    qkv_grad_parts, e_one_parts, query_parts = [], [], []
    for number, ((start, size, first_key, last), log_part, gate) in enumerate(
        zip(reversed(list(spans(token_count))), reversed(log_total), gates)
    ):
        grad_block = tie(grad_grouped[start : start + size], *gate)
        if number == 2:
            grad_block = tie(grad_block, e_one_parts[0])
        if number == 3:
            chip_late = chip_rows(e_one_parts[0])
            grad_block = tie(grad_block, chip_late)
        query_part, key_part, value_part = block_backward(
            grouped[start : start + size],
            key_low[first_key:last],
            value_seq[first_key:last],
            log_part,
            grad_block,
            segment_row,
            start,
            first_key,
        )
        key_grad = key_grad.at[first_key:last].add(key_part)
        value_grad = value_grad.at[first_key:last].add(value_part)
        query_parts.insert(0, query_part)
        if number % 2 == 1:
            span = slice(start, start + half_rows)
            cosine_span, sine_span = cosine_wide[span], -sine_wide[span]
            query_grad = jnp.concatenate(query_parts, axis=0).reshape(half_rows, -1, HD)
            qkv_grad_part = jnp.concatenate(
                [
                    rotate(query_grad, cosine_span, sine_span).reshape(half_rows, -1),
                    rotate(key_grad[span], cosine_span, sine_span).reshape(half_rows, -1),
                    value_grad[span].reshape(half_rows, -1),
                ],
                axis=1,
            ).astype(BF)
            query_parts = []
            qkv_grad_parts.insert(0, qkv_grad_part)
            if number == 1:
                e_one_parts.append(dot_cols(qkv_grad_part, qkv_full, BF))
    qkv_weight_grad = dot_rows(normed, jnp.concatenate(qkv_grad_parts, axis=0), BF)
    e_one_parts.append(dot_cols(tie(qkv_grad_parts[0], qkv_weight_grad), qkv_full, BF))

    chip_early = chip_rows(e_one_parts[1])

    qkv_cut = qkv_weight_grad.reshape(groups, 2, rows, -1)

    def qkv_pick(side):
        def pick(back):
            start = ((z_index - back) % groups, side, 0, 0)
            return lax.dynamic_slice(qkv_cut, start, (1, 1, rows, qkv_cols))[0, 0]

        return pick

    qkv_mine, qkv_other_y = qkv_pick(y_index), qkv_pick(1 - y_index)
    qkv_sent = [swap_y(qkv_other_y(back)) for back in range(1, groups + 1)]

    def qkv_part(back):
        return two_way(qkv_mine(back), qkv_sent[back - 1])

    def tokens_rows(chip_sum, chip_other, start):
        e_one = two_way(chip_sum, chip_other)
        grad_rows = lax.dynamic_slice_in_dim(
            hidden_low, (t_index ^ (start // quarter + core_index)) * quarter, quarter, 0
        ).astype(F32)
        root = core_rows(token_root, start, core_index)
        n_one = core_rows(tokens, start, core_index).astype(F32) * root
        own = grad_rows + root * (e_one - n_one * jnp.mean(e_one * n_one, axis=-1, keepdims=True))
        own = own.astype(BF)
        return own, swap_core(own)

    def core_order(own, other):
        return jnp.where(
            core_index == 0,
            jnp.concatenate([own, other], axis=0),
            jnp.concatenate([other, own], axis=0),
        ).astype(F32)

    late_other, early_other = swap_x(chip_late), swap_x(chip_early)
    layer_x = swap_x(layer_quarter)
    layer_output = absolute(
        [layer_quarter, swap_core(layer_quarter), layer_x, swap_core(tie(layer_x, qkv_weight_grad))],
        BF,
    )
    qkv_send = tie(qkv_part(1).astype(BF), chip_early, out_block)
    qkv_runs = []
    for step in range(1, groups):
        qkv_runs.append(hop(qkv_send))
        if step == 1:
            late_rows = tokens_rows(chip_late, tie(late_other, qkv_send), half_rows)
        if step < groups - 1:
            qkv_send = (qkv_runs[-1].astype(F32) + qkv_part(step + 1)).astype(BF)
            if step == 1:
                qkv_send = tie(qkv_send, gu_trade_b[1])
                early_rows = tokens_rows(chip_early, tie(early_other, qkv_send), 0)
    tokens_grad = jnp.concatenate(
        [core_order(*early_rows), core_order(tie(late_rows[0], qkv_send), late_rows[1])], axis=0
    )
    qkv_block = ring_end(tie(qkv_runs[-1], tokens_grad), qkv_part)

    def all_units(pairs, place):
        pairs = [(mine, tie(got, qkv_send)) for mine, got in pairs]

        def side(which):
            return jnp.concatenate(
                [pair[which][:, place * n : (place + 1) * n] for pair, n in zip(pairs, part_units)],
                axis=1,
            )

        return by_y(side(0), side(1), 1).astype(F32)

    gate_g, up_g = all_units((gu_trade_a, gu_trade_b), 0), all_units((gu_trade_a, gu_trade_b), 1)
    down_weight_grad = all_units((down_trade_a, down_trade_b), 0).T

    attn_gain_part = jnp.sum(
        qkv_block * jnp.concatenate([query_weight, key_weight, value_weight], axis=1).astype(F32),
        axis=1,
    )
    ffn_gain_part = jnp.sum(
        gate_g * gate_weight.astype(F32) + up_g * up_weight.astype(F32), axis=1
    )

    def sum_tensor(value):
        value = value + swap_core(value)
        return value + swap_x(value)

    attn_gain_grad, ffn_gain_grad = sum_tensor(jnp.stack([attn_gain_part, ffn_gain_part]))
    qkv_out = qkv_block * attn_scale
    return (
        layer_output,
        tokens_grad,
        attn_gain_grad,
        qkv_out[:, :q_cols],
        qkv_out[:, q_cols : q_cols + kv_cols],
        qkv_out[:, q_cols + kv_cols :],
        out_grad,
        ffn_gain_grad,
        gate_g * ffn_scale,
        up_g * ffn_scale,
        down_weight_grad,
    )


def solution(mesh):
    return jax.shard_map(
        partial(shards, mesh.shape["dp"], mesh.shape["tensor"]),
        mesh=mesh,
        in_specs=(
            P("dp", None),
            P("dp", None),
            P("dp"),
            P("dp", "tensor"),
            P("dp", "tensor"),
            P("dp", "tensor"),
            P("tensor", "dp"),
            P("dp"),
            P("dp", "tensor"),
            P("dp", "tensor"),
            P("tensor", "dp"),
            P("dp", None),
        ),
        out_specs=(
            P("dp", None),
            P("dp", None),
            P("dp"),
            P("dp", "tensor"),
            P("dp", "tensor"),
            P("dp", "tensor"),
            P("tensor", "dp"),
            P("dp"),
            P("dp", "tensor"),
            P("dp", "tensor"),
            P("tensor", "dp"),
        ),
        check_vma=False,
    )
```
